32 devices in a mesh: dp: 8 (over y, x, core), tensor: 4 (over z).
Axes of the slice: x: 2, y: 2, z: 4, core: 2. Of those that a mesh axis runs over, the one named last changes fastest.
Arguments:
- tokens: bfloat16 [8192, 2048], P(('dp', 'tensor')), may hold values from -6 to 6
- w_query: bfloat16 [2048, 2048], P('dp', 'tensor'), may hold values from -1 to 1
- w_key: bfloat16 [2048, 2048], P('dp', 'tensor'), may hold values from -1 to 1
- w_value: bfloat16 [2048, 2048], P('dp', 'tensor'), may hold values from -0.125 to 0.125
- w_out: bfloat16 [2048, 2048], P('tensor', 'dp'), may hold values from -0.125 to 0.125
- w_gate: bfloat16 [2048, 8192], P('dp', 'tensor'), may hold values from -0.125 to 0.125
- w_up: bfloat16 [2048, 8192], P('dp', 'tensor'), may hold values from -0.125 to 0.125
- w_down: bfloat16 [8192, 2048], P('tensor', 'dp'), may hold values from -0.0625 to 0.0625
- query_gain: bfloat16 [16, 128], P('tensor', 'dp'), may hold values from 0.8 to 1.2
- key_gain: bfloat16 [16, 128], P('tensor', 'dp'), may hold values from 0.8 to 1.2
- attn_gain: bfloat16 [2048], P('dp'), may hold values from 0.5 to 1.5
- mlp_gain: bfloat16 [2048], P('dp'), may hold values from 0.5 to 1.5
- cotangent: bfloat16 [8192, 2048], P(('dp', 'tensor')), may hold values from -6 to 6
Outputs:
- layer_output: bfloat16 [8192, 2048], P(('dp', 'tensor'))
- grad_tokens: float32 [8192, 2048], P(('dp', 'tensor'))
- grad_w_query: float32 [2048, 2048], P('dp', 'tensor')
- grad_w_key: float32 [2048, 2048], P('dp', 'tensor')
- grad_w_value: float32 [2048, 2048], P('dp', 'tensor')
- grad_w_out: float32 [2048, 2048], P('tensor', 'dp')
- grad_w_gate: float32 [2048, 8192], P('dp', 'tensor')
- grad_w_up: float32 [2048, 8192], P('dp', 'tensor')
- grad_w_down: float32 [8192, 2048], P('tensor', 'dp')
- grad_query_gain: float32 [16, 128], P('tensor', 'dp')
- grad_key_gain: float32 [16, 128], P('tensor', 'dp')
- grad_attn_gain: float32 [2048], P('dp')
- grad_mlp_gain: float32 [2048], P('dp')
The draws below stay inside these ranges and needn't reach their ends.
All inputs are finite; a program needn't handle non-finite values.
Results may differ from the reference program's by a relative error of at most 0.015.
Values may be sent and summed in bfloat16 or wider, within the bound.
No kernel may reach another device: no remote copies, remote signals or barrier semaphores. Data moves between devices by JAX's collectives and lax.ppermute only.
A program may use at most 320 MiB of HBM per device.

```python
import math
import jax
import jax.numpy as jnp
from jax import lax

D = 2048
HEADS = 16
HD = 128
FF = 8192
SEQLEN = 1024
TOKENS = 8192
N_DP = 8


def weight_draw(key, salt):
    scale_factor = 1.0 / math.sqrt(D)
    values = jnp.clip(jax.random.normal(jax.random.fold_in(key, salt), (D, D), jnp.float32), -6.0, 6.0)
    return values * scale_factor


def draw_w_query(key, part):
    return weight_draw(key, 11).astype(jnp.bfloat16)


def draw_w_key(key, part):
    return weight_draw(key, 12).astype(jnp.bfloat16)


def gain_field(key, salt):
    noise = jax.random.uniform(jax.random.fold_in(key, salt), (HEADS, HD), jnp.float32, -1.0, 1.0)
    base_gain = 1.0 + 0.15 * noise
    return base_gain


def draw_query_gain(key, part):
    return gain_field(key, 21).astype(jnp.bfloat16)


def draw_key_gain(key, part):
    return gain_field(key, 31).astype(jnp.bfloat16)


def shard_levels(rng, shape, split, least, largest):
    level = 1.0
    for axis_at, parts in split:
        draws = jax.random.uniform(jax.random.fold_in(jax.random.fold_in(rng, 6), axis_at), (parts,), jnp.float32, least / len(split), largest / len(split))
        level = level * jnp.repeat(jnp.exp(draws), shape[axis_at] // parts).reshape((-1,) + (1,) * (len(shape) - 1 - axis_at))
    return level


def normal_values(rng, shape, width, limit, shards=(), kind=jnp.bfloat16):
    entries = jax.random.normal(rng, shape, jnp.float32) * width
    if len(shards) > 0:
        entries = shard_levels(rng, shape, shards, -0.22, 0.18) * entries
    return jnp.clip(entries, min=-limit, max=limit).astype(kind)


def setup_inputs(seed: int = 0) -> dict:
    arg_keys = jax.random.split(jax.random.key(seed), 14)
    return {
        "tokens": normal_values(arg_keys[0], (TOKENS, D), 1.0, 6.0, ((0, 32),)),
        "w_query": draw_w_query(jax.random.fold_in(arg_keys[13], 71), 0),
        "w_key": draw_w_key(jax.random.fold_in(arg_keys[13], 71), 0),
        "w_value": normal_values(arg_keys[3], (D, D), D ** -0.5, 0.125, ((0, 8), (1, 4))),
        "w_out": normal_values(arg_keys[4], (D, D), D ** -0.5, 0.125, ((0, 4), (1, 8))),
        "w_gate": normal_values(arg_keys[5], (D, FF), D ** -0.5, 0.125, ((0, 8), (1, 4))),
        "w_up": normal_values(arg_keys[6], (D, FF), D ** -0.5, 0.125, ((0, 8), (1, 4))),
        "w_down": normal_values(arg_keys[7], (FF, D), FF ** -0.5, 0.0625, ((0, 4), (1, 8))),
        "query_gain": draw_query_gain(jax.random.fold_in(arg_keys[13], 71), 0),
        "key_gain": draw_key_gain(jax.random.fold_in(arg_keys[13], 71), 0),
        "attn_gain": jnp.clip(1.0 + 0.1 * jax.random.normal(arg_keys[10], (D,), jnp.float32), 0.5, 1.5).astype(jnp.bfloat16),
        "mlp_gain": jnp.clip(1.0 + 0.1 * jax.random.normal(arg_keys[11], (D,), jnp.float32), 0.5, 1.5).astype(jnp.bfloat16),
        "cotangent": normal_values(arg_keys[12], (TOKENS, D), 1.0, 6.0, ((0, 32),)),
    }


rope_theta = 500000.0
norm_eps = 1e-06
top_prec = lax.Precision.HIGHEST

def rope_tables(length, head_size):
    half_size = head_size // 2
    freqs = rope_theta ** (-(jnp.arange(half_size, dtype=jnp.float32) * 2.0) / head_size)
    angles = jnp.arange(length, dtype=jnp.float32)[:, None] * freqs[None, :]
    return (jnp.cos(angles), jnp.sin(angles))

def rotate(values_in, cosine, sine_tab):
    half_size = values_in.shape[-1] // 2
    first_half = values_in[..., :half_size]
    second_half = values_in[..., half_size:]
    cos_b = cosine[:, None, :]
    sin_b = sine_tab[:, None, :]
    return jnp.concatenate([first_half * cos_b - second_half * sin_b, second_half * cos_b + first_half * sin_b], axis=-1)

def unrotate(values_in, cosine, sine_tab):
    half_size = values_in.shape[-1] // 2
    first_half = values_in[..., :half_size]
    second_half = values_in[..., half_size:]
    cos_b = cosine[:, None, :]
    sin_b = sine_tab[:, None, :]
    return jnp.concatenate([first_half * cos_b + second_half * sin_b, second_half * cos_b - first_half * sin_b], axis=-1)

def contract_rows(left_op, right_op):
    return lax.dot_general(left_op, right_op, (((0,), (0,)), ((), ())), preferred_element_type=jnp.float32)

def contract_cols(left_op, right_op):
    return lax.dot_general(left_op, right_op, (((1,), (1,)), ((), ())), preferred_element_type=jnp.float32)

def one_sequence(sequence, cot_rows, params):
    w_query, w_key, w_value, w_out, w_gate, w_up, w_down, query_gain, key_gain, attn_gain, mlp_gain = params
    length = sequence.shape[0]
    model_width = sequence.shape[1]
    head_count = query_gain.shape[0]
    head_size = query_gain.shape[1]
    query_raw = jnp.dot(sequence, w_query, preferred_element_type=jnp.float32)
    key_raw = jnp.dot(sequence, w_key, preferred_element_type=jnp.float32)
    value_raw = jnp.dot(sequence, w_value, preferred_element_type=jnp.float32)
    query_rs = lax.rsqrt(lax.optimization_barrier(jnp.mean(query_raw * query_raw, axis=1, keepdims=True)) + norm_eps)
    key_rs = lax.rsqrt(lax.optimization_barrier(jnp.mean(key_raw * key_raw, axis=1, keepdims=True)) + norm_eps)
    query_hat = query_raw * query_rs
    key_hat = key_raw * key_rs
    query_norm = query_hat.reshape(length, head_count, head_size) * query_gain.astype(jnp.float32)[None]
    key_norm = key_hat.reshape(length, head_count, head_size) * key_gain.astype(jnp.float32)[None]
    cosine, sine_tab = rope_tables(length, head_size)
    query_rot = rotate(query_norm, cosine, sine_tab).astype(jnp.bfloat16)
    key_rot = rotate(key_norm, cosine, sine_tab).astype(jnp.bfloat16)
    value_heads = value_raw.reshape(length, head_count, head_size).astype(jnp.bfloat16)
    score_scale = 1.0 / math.sqrt(head_size)
    allowed = jnp.arange(length)[:, None] >= jnp.arange(length)[None, :]
    scores = jnp.einsum('qhd,khd->hqk', query_rot.astype(jnp.float32), key_rot.astype(jnp.float32), precision=top_prec) * score_scale
    scores = jnp.where(allowed[None], scores, -1e+30)
    row_max = lax.optimization_barrier(jnp.max(scores, axis=2, keepdims=True))
    exp_scores = jnp.exp(scores - row_max)
    row_sum = lax.optimization_barrier(jnp.sum(exp_scores, axis=2, keepdims=True))
    soft_probs = (exp_scores / row_sum).astype(jnp.bfloat16)
    log_sums = row_max + jnp.log(row_sum)
    context = jnp.einsum('hqk,khd->qhd', soft_probs.astype(jnp.float32), value_heads.astype(jnp.float32), precision=top_prec)
    context = context.reshape(length, model_width).astype(jnp.bfloat16)
    attn_part = jnp.dot(context, w_out, preferred_element_type=jnp.float32)
    attn_rs = lax.rsqrt(lax.optimization_barrier(jnp.mean(attn_part * attn_part, axis=1, keepdims=True)) + norm_eps)
    attn_hat = attn_part * attn_rs
    residual = sequence.astype(jnp.float32) + attn_hat * attn_gain.astype(jnp.float32)
    middle = residual.astype(jnp.bfloat16)
    gate_pre = jnp.dot(middle, w_gate, preferred_element_type=jnp.float32)
    up_pre = jnp.dot(middle, w_up, preferred_element_type=jnp.float32)
    gate_sig = jax.nn.sigmoid(gate_pre)
    hidden = (gate_pre * gate_sig * up_pre).astype(jnp.bfloat16)
    mlp_part = jnp.dot(hidden, w_down, preferred_element_type=jnp.float32)
    mlp_rs = lax.rsqrt(lax.optimization_barrier(jnp.mean(mlp_part * mlp_part, axis=1, keepdims=True)) + norm_eps)
    mlp_hat = mlp_part * mlp_rs
    layer_output = (residual + mlp_hat * mlp_gain.astype(jnp.float32)).astype(jnp.bfloat16)
    upstream = cot_rows.astype(jnp.float32)
    grad_mlp_gain = lax.optimization_barrier(jnp.sum(upstream * mlp_hat, axis=0))
    d_mlp_norm = upstream * mlp_gain.astype(jnp.float32)
    d_mlp = (mlp_rs * (d_mlp_norm - mlp_hat * lax.optimization_barrier(jnp.mean(d_mlp_norm * mlp_hat, axis=1, keepdims=True)))).astype(jnp.bfloat16)
    d_hidden = contract_cols(d_mlp, w_down)
    grad_w_down = contract_rows(hidden, d_mlp)
    d_up = (d_hidden * gate_pre * gate_sig).astype(jnp.bfloat16)
    d_gate = (d_hidden * up_pre * gate_sig * (1.0 + gate_pre * (1.0 - gate_sig))).astype(jnp.bfloat16)
    grad_w_gate = contract_rows(middle, d_gate)
    grad_w_up = contract_rows(middle, d_up)
    d_residual = upstream + contract_cols(d_gate, w_gate) + contract_cols(d_up, w_up)
    grad_attn_gain = lax.optimization_barrier(jnp.sum(d_residual * attn_hat, axis=0))
    d_attn_norm = d_residual * attn_gain.astype(jnp.float32)
    d_attn = (attn_rs * (d_attn_norm - attn_hat * lax.optimization_barrier(jnp.mean(d_attn_norm * attn_hat, axis=1, keepdims=True)))).astype(jnp.bfloat16)
    d_context = contract_cols(d_attn, w_out).astype(jnp.bfloat16)
    grad_w_out = contract_rows(context, d_attn)
    d_context_heads = d_context.reshape(length, head_count, head_size).astype(jnp.float32)
    context_heads = context.reshape(length, head_count, head_size).astype(jnp.float32)
    probs_full = jnp.exp(scores - log_sums)
    probs_round = probs_full.astype(jnp.bfloat16).astype(jnp.float32)
    d_value = jnp.einsum('hqk,qhd->khd', probs_round, d_context_heads, precision=top_prec)
    d_probs = jnp.einsum('qhd,khd->hqk', d_context_heads, value_heads.astype(jnp.float32), precision=top_prec)
    row_delta = jnp.einsum('qhd,qhd->hq', d_context_heads, context_heads, precision=top_prec)
    d_scores = (probs_full * (d_probs - row_delta[..., None]) * score_scale).astype(jnp.bfloat16).astype(jnp.float32)
    d_query_rot = jnp.einsum('hqk,khd->qhd', d_scores, key_rot.astype(jnp.float32), precision=top_prec)
    d_key_rot = jnp.einsum('hqk,qhd->khd', d_scores, query_rot.astype(jnp.float32), precision=top_prec)
    d_query_norm = unrotate(d_query_rot, cosine, sine_tab)
    d_key_norm = unrotate(d_key_rot, cosine, sine_tab)
    grad_query_gain = lax.optimization_barrier(jnp.sum(d_query_norm * query_hat.reshape(length, head_count, head_size), axis=0))
    grad_key_gain = lax.optimization_barrier(jnp.sum(d_key_norm * key_hat.reshape(length, head_count, head_size), axis=0))
    d_query_hat = (d_query_norm * query_gain.astype(jnp.float32)[None]).reshape(length, model_width)
    d_key_hat = (d_key_norm * key_gain.astype(jnp.float32)[None]).reshape(length, model_width)
    d_query = (query_rs * (d_query_hat - query_hat * lax.optimization_barrier(jnp.mean(d_query_hat * query_hat, axis=1, keepdims=True)))).astype(jnp.bfloat16)
    d_key = (key_rs * (d_key_hat - key_hat * lax.optimization_barrier(jnp.mean(d_key_hat * key_hat, axis=1, keepdims=True)))).astype(jnp.bfloat16)
    d_value_b = d_value.reshape(length, model_width).astype(jnp.bfloat16)
    grad_tokens = d_residual + contract_cols(d_query, w_query) + contract_cols(d_key, w_key) + contract_cols(d_value_b, w_value)
    grad_w_query = contract_rows(sequence, d_query)
    grad_w_key = contract_rows(sequence, d_key)
    grad_w_value = contract_rows(sequence, d_value_b)
    grads = (grad_w_query, grad_w_key, grad_w_value, grad_w_out, grad_w_gate, grad_w_up, grad_w_down, grad_query_gain, grad_key_gain, grad_attn_gain, grad_mlp_gain)
    return (layer_output, grad_tokens, grads)

def reference(tokens, w_query, w_key, w_value, w_out, w_gate, w_up, w_down, query_gain, key_gain, attn_gain, mlp_gain, cotangent):
    params = (w_query, w_key, w_value, w_out, w_gate, w_up, w_down, query_gain, key_gain, attn_gain, mlp_gain)
    sequences = tokens.reshape(N_DP, SEQLEN, D)
    cot_seqs = cotangent.reshape(N_DP, SEQLEN, D)
    initial = jax.tree.map(lambda weight: jnp.zeros(weight.shape, jnp.float32), params)

    def step_fn(carry, pair):
        layer_output, grad_tokens, grads = one_sequence(pair[0], pair[1], params)
        return (jax.tree.map(jnp.add, carry, grads), (layer_output, grad_tokens))
    totals, stacked = lax.scan(step_fn, initial, (sequences, cot_seqs))
    outputs = stacked[0].reshape(TOKENS, D)
    d_inputs = stacked[1].reshape(TOKENS, D)
    return (outputs, d_inputs, totals[0], totals[1], totals[2], totals[3], totals[4], totals[5], totals[6], totals[7], totals[8], totals[9], totals[10])
```

```python
import functools
import math

import jax
import jax.numpy as jnp
from jax import lax
from jax.experimental import pallas as pl
from jax.experimental.pallas import tpu as pltpu
from jax.sharding import PartitionSpec as P

rope_theta = 500000.0
norm_eps = 1e-06

F32 = jnp.float32
BF16 = jnp.bfloat16

PAIRS = [(0, 1), (1, 0), (2, 3), (3, 2)]
MIDDLE = [(1, 2), (2, 1)]
OUTWARD = [(2, 3), (1, 0)]
INWARD = [(3, 2), (0, 1)]

ORDER_A = (0, 2, 4, 6, 1, 3, 5, 7)
SWAP_B = (0, 2, 1, 3, 4, 6, 5, 7)
BLOCKS = 8
BIT_CORE, BIT_X, BIT_Y = 1, 2, 4


def rope_tables(length, head_size):
    half_size = head_size // 2
    freqs = rope_theta ** (-(jnp.arange(half_size, dtype=F32) * 2.0) / head_size)
    angles = jnp.arange(length, dtype=F32)[:, None] * freqs[None, :]
    cosine, sine = jnp.cos(angles), jnp.sin(angles)
    return (
        jnp.concatenate([cosine, cosine], axis=1),
        jnp.concatenate([-sine, sine], axis=1),
    )


def shift(value, pairs):
    return lax.ppermute(value, "tensor", pairs)


def line_gather(own):
    e1 = shift(own, PAIRS)
    m_own = shift(own, MIDDLE)
    m_e1 = shift(e1, MIDDLE)
    f_own = shift(m_own, OUTWARD)
    f_e1 = shift(m_e1, OUTWARD)
    return own, e1, m_own + f_own, m_e1 + f_e1


def line_scatter(own, p1, p2, p3):
    b3 = shift(p3, INWARD)
    b2 = shift(p2, INWARD)
    m3 = shift(p3 + b3, MIDDLE)
    m2 = shift(p2 + b2, MIDDLE)
    e1 = shift(p1 + m3, PAIRS)
    return own + e1.astype(F32) + m2.astype(F32)


def flip(value, bit):
    return lax.ppermute(value, "dp", [(i, i ^ bit) for i in range(8)])


def dot(a, b, dims=((1,), (0,)), out=F32):
    return lax.dot_general(a, b, (dims, ((), ())), preferred_element_type=F32).astype(out)


COLS = ((1,), (1,))
ROWS = ((0,), (0,))


def qkv_body(count, xord_ref, bidx_ref, *refs):
    xs = refs[:count]
    alo, ahi, blo, bhi, _, _, _, qk_ref, v_ref, sq_ref, acc = refs[count:]
    step = pl.program_id(0)
    half = alo.shape[2]

    def add(a_ref, b_ref, first):
        for i in range(count):
            x = xs[i][...]
            for w_ref, lo in ((a_ref, 0), (b_ref, half)):
                part = jnp.dot(x, w_ref[0], preferred_element_type=F32)
                if first:
                    acc[i, :, lo : lo + half] = part
                else:
                    acc[i, :, lo : lo + half] += part

    @pl.when(step == 0)
    def _():
        add(alo, blo, True)

    @pl.when((step > 0) & (step < BLOCKS // 2))
    def _():
        add(alo, blo, False)

    @pl.when(step >= BLOCKS // 2)
    def _():
        add(ahi, bhi, False)

    @pl.when(step == BLOCKS - 1)
    def _():
        width = qk_ref.shape[2] // 2
        lane = lax.broadcasted_iota(jnp.int32, sq_ref.shape[1:], 1)
        for i in range(count):
            qk = acc[i, :, : 2 * width]
            qk_ref[i] = qk
            v_ref[i] = acc[i, :, 2 * width :].astype(BF16)
            sq = qk * qk
            q_sum = jnp.sum(sq[:, :width], axis=1, keepdims=True)
            k_sum = jnp.sum(sq[:, width:], axis=1, keepdims=True)
            sq_ref[i] = jnp.where(lane == 0, q_sum, jnp.where(lane == 1, k_sum, 0.0))


def qkv_call(xs, weights, xord, bidx, start, prev, width):
    count = len(xs)
    rows, model = xs[0].shape
    kb = model // BLOCKS
    half = weights[0].shape[2]
    lo = lambda j, xo, bi: (jnp.minimum(j, BLOCKS // 2 - 1), 0, 0)
    hi = lambda j, xo, bi: (jnp.maximum(j - BLOCKS // 2, 0), 0, 0)
    lob = lambda j, xo, bi: (bi[jnp.minimum(j, BLOCKS // 2 - 1)], 0, 0)
    hib = lambda j, xo, bi: (bi[jnp.maximum(j, BLOCKS // 2)] - BLOCKS // 2, 0, 0)
    at = start // count
    out = lambda j, xo, bi: (at, 0, 0)
    shapes = (
        jax.ShapeDtypeStruct((4, rows, 2 * width), F32),
        jax.ShapeDtypeStruct((4, rows, width), BF16),
        jax.ShapeDtypeStruct((4, rows, 128), F32),
    )
    if prev is None:
        prev = tuple(jnp.zeros((8, 128), s.dtype) for s in shapes)
        alias = {}
    else:
        alias = {count + 6 + i: i for i in range(3)}
    return pl.pallas_call(
        functools.partial(qkv_body, count),
        out_shape=shapes,
        grid_spec=pltpu.PrefetchScalarGridSpec(
            num_scalar_prefetch=2,
            grid=(BLOCKS,),
            in_specs=[pl.BlockSpec((rows, kb), lambda j, xo, bi: (0, xo[j]))] * count
            + [
                pl.BlockSpec((1, kb, half), lo),
                pl.BlockSpec((1, kb, half), hi),
                pl.BlockSpec((1, kb, half), lob),
                pl.BlockSpec((1, kb, half), hib),
            ]
            + [pl.BlockSpec(memory_space=pl.ANY)] * 3,
            out_specs=[
                pl.BlockSpec((count, rows, 2 * width), out),
                pl.BlockSpec((count, rows, width), out),
                pl.BlockSpec((count, rows, 128), out),
            ],
            scratch_shapes=[pltpu.VMEM((count, rows, 3 * width), F32)],
        ),
        input_output_aliases=alias,
        compiler_params=pltpu.CompilerParams(dimension_semantics=("arbitrary",)),
        name="qkv",
    )(xord, bidx, *xs, *weights, *prev)


def attn_fwd_body(
    scale,
    inv_ref,
    q_ref,
    k_ref,
    v_ref,
    rq_ref,
    rk_ref,
    gq_ref,
    gk_ref,
    cos_ref,
    sin_ref,
    qrot_ref,
    krot_ref,
    ctx_ref,
    lse_ref,
):
    rows, head = q_ref.shape[1:]
    gq, gk = gq_ref[0], gk_ref[0]
    for b in range(4):
        r = inv_ref[b]
        cos = cos_ref[b * rows : (b + 1) * rows]
        sin = sin_ref[b * rows : (b + 1) * rows]
        qn = q_ref[r] * rq_ref[r] * gq
        kn = k_ref[r] * rk_ref[r] * gk
        qrot_ref[r] = (qn * cos + pltpu.roll(qn, head // 2, 1) * sin).astype(BF16)
        krot_ref[r] = (kn * cos + pltpu.roll(kn, head // 2, 1) * sin).astype(BF16)
    causal = lax.broadcasted_iota(jnp.int32, (rows, rows), 0) >= lax.broadcasted_iota(
        jnp.int32, (rows, rows), 1
    )
    for b in range(4):
        r = inv_ref[b]
        q = qrot_ref[r]
        parts = []
        for c in range(b + 1):
            s = dot(q, krot_ref[inv_ref[c]], COLS) * scale
            if c == b:
                s = jnp.where(causal, s, -1e30)
            parts.append(s)
        top = jnp.max(parts[0], axis=1, keepdims=True)
        for s in parts[1:]:
            top = jnp.maximum(top, jnp.max(s, axis=1, keepdims=True))
        exps = [jnp.exp(s - top) for s in parts]
        total = jnp.sum(exps[0], axis=1, keepdims=True)
        for e in exps[1:]:
            total = total + jnp.sum(e, axis=1, keepdims=True)
        inverse = 1.0 / total
        ctx = None
        for c in range(b + 1):
            part = jnp.dot(
                (exps[c] * inverse).astype(BF16), v_ref[inv_ref[c]], preferred_element_type=F32
            )
            ctx = part if ctx is None else ctx + part
        ctx_ref[r] = ctx.astype(BF16)
        lse_ref[0, r] = top + jnp.log(total)


def attn_fwd(inv, qk, v, rq, rk, gq, gk, cos, sin):
    _, rows, width2 = qk.shape
    width = width2 // 2
    heads, _, head = gq.shape
    per_head = pl.BlockSpec((4, rows, head), lambda h, iv: (0, 0, h))
    return pl.pallas_call(
        functools.partial(attn_fwd_body, 1.0 / math.sqrt(head)),
        out_shape=(
            jax.ShapeDtypeStruct((4, rows, width), BF16),
            jax.ShapeDtypeStruct((4, rows, width), BF16),
            jax.ShapeDtypeStruct((4, rows, width), BF16),
            jax.ShapeDtypeStruct((heads, 4, rows, 1), F32),
        ),
        grid_spec=pltpu.PrefetchScalarGridSpec(
            num_scalar_prefetch=1,
            grid=(heads,),
            in_specs=[
                per_head,
                pl.BlockSpec((4, rows, head), lambda h, iv: (0, 0, heads + h)),
                per_head,
                pl.BlockSpec((4, rows, 1), lambda h, iv: (0, 0, 0)),
                pl.BlockSpec((4, rows, 1), lambda h, iv: (0, 0, 0)),
                pl.BlockSpec((1, 1, head), lambda h, iv: (h, 0, 0)),
                pl.BlockSpec((1, 1, head), lambda h, iv: (h, 0, 0)),
                pl.BlockSpec(cos.shape, lambda h, iv: (0, 0)),
                pl.BlockSpec(sin.shape, lambda h, iv: (0, 0)),
            ],
            out_specs=[
                per_head,
                per_head,
                per_head,
                pl.BlockSpec((1, 4, rows, 1), lambda h, iv: (h, 0, 0, 0)),
            ],
        ),
        compiler_params=pltpu.CompilerParams(dimension_semantics=("arbitrary",)),
        name="attn_fwd",
    )(inv, qk, qk, v, rq, rk, gq, gk, cos, sin)


def attn_bwd_body(
    scale,
    inv_ref,
    qrot_ref,
    krot_ref,
    v_ref,
    dctx_ref,
    ctx_ref,
    lse_ref,
    q_ref,
    k_ref,
    rq_ref,
    rk_ref,
    gq_ref,
    gk_ref,
    cos_ref,
    sin_ref,
    dq_ref,
    dk_ref,
    dv_ref,
    gain_ref,
    dots_ref,
    dk_acc,
    dv_acc,
):
    rows, head = q_ref.shape[1:]
    causal = lax.broadcasted_iota(jnp.int32, (rows, rows), 0) >= lax.broadcasted_iota(
        jnp.int32, (rows, rows), 1
    )
    lane = lax.broadcasted_iota(jnp.int32, (rows, 128), 1)
    gq, gk = gq_ref[0], gk_ref[0]
    first = pl.program_id(0) == 0

    def finish(raw, b, r, raw_ref, rs_ref, gain, out_ref):
        cos = cos_ref[b * rows : (b + 1) * rows]
        sin = sin_ref[b * rows : (b + 1) * rows]
        norm = raw * cos - pltpu.roll(raw, head // 2, 1) * sin
        hat = raw_ref[r] * rs_ref[r]
        both = norm * hat
        scaled = norm * gain
        out_ref[r] = scaled
        return (
            jnp.sum(both, axis=0, keepdims=True),
            jnp.sum(both * gain, axis=1, keepdims=True),
        )

    q_gain = jnp.zeros((1, head), F32)
    k_gain = jnp.zeros((1, head), F32)
    q_dots = []
    for b in range(4):
        r = inv_ref[b]
        q = qrot_ref[r]
        dctx = dctx_ref[r]
        lse = lse_ref[0, r]
        delta = jnp.sum(dctx.astype(F32) * ctx_ref[r].astype(F32), axis=1, keepdims=True)
        dq = None
        for c in range(b + 1):
            rc = inv_ref[c]
            k = krot_ref[rc]
            s = dot(q, k, COLS) * scale
            if c == b:
                s = jnp.where(causal, s, -1e30)
            p = jnp.exp(s - lse)
            dp = dot(dctx, v_ref[rc], COLS)
            ds = (p * (dp - delta) * scale).astype(BF16)
            dv_part = dot(p.astype(BF16), dctx, ROWS)
            dk_part = dot(ds, q, ROWS)
            dq_part = jnp.dot(ds, k, preferred_element_type=F32)
            dq = dq_part if dq is None else dq + dq_part
            if c == b:
                dv_acc[c] = dv_part
                dk_acc[c] = dk_part
            else:
                dv_acc[c] += dv_part
                dk_acc[c] += dk_part
        gain_part, row_dot = finish(dq, b, r, q_ref, rq_ref, gq, dq_ref)
        q_gain = q_gain + gain_part
        q_dots.append(row_dot)
    for b in range(4):
        r = inv_ref[b]
        gain_part, row_dot = finish(dk_acc[b], b, r, k_ref, rk_ref, gk, dk_ref)
        k_gain = k_gain + gain_part
        dv_ref[r] = dv_acc[b].astype(BF16)
        old = jnp.where(first, 0.0, dots_ref[r])
        dots_ref[r] = old + jnp.where(
            lane == 0, q_dots[b], jnp.where(lane == 1, row_dot, 0.0)
        )
    row = lax.broadcasted_iota(jnp.int32, (8, head), 0)
    gain_ref[0] = jnp.where(row == 0, q_gain, jnp.where(row == 1, k_gain, 0.0))


def attn_bwd(inv, qrot, krot, v, dctx, ctx, lse, qk, rq, rk, gq, gk, cos, sin):
    _, rows, width = qrot.shape
    heads, _, head = gq.shape
    per_head = pl.BlockSpec((4, rows, head), lambda h, iv: (0, 0, h))
    column = pl.BlockSpec((4, rows, 1), lambda h, iv: (0, 0, 0))
    gain = pl.BlockSpec((1, 1, head), lambda h, iv: (h, 0, 0))
    return pl.pallas_call(
        functools.partial(attn_bwd_body, 1.0 / math.sqrt(head)),
        out_shape=(
            jax.ShapeDtypeStruct((4, rows, width), F32),
            jax.ShapeDtypeStruct((4, rows, width), F32),
            jax.ShapeDtypeStruct((4, rows, width), BF16),
            jax.ShapeDtypeStruct((heads, 8, head), F32),
            jax.ShapeDtypeStruct((4, rows, 128), F32),
        ),
        grid_spec=pltpu.PrefetchScalarGridSpec(
            num_scalar_prefetch=1,
            grid=(heads,),
            in_specs=[
                per_head,
                per_head,
                per_head,
                per_head,
                per_head,
                pl.BlockSpec((1, 4, rows, 1), lambda h, iv: (h, 0, 0, 0)),
                per_head,
                pl.BlockSpec((4, rows, head), lambda h, iv: (0, 0, heads + h)),
                column,
                column,
                gain,
                gain,
                pl.BlockSpec(cos.shape, lambda h, iv: (0, 0)),
                pl.BlockSpec(sin.shape, lambda h, iv: (0, 0)),
            ],
            out_specs=[
                per_head,
                per_head,
                per_head,
                pl.BlockSpec((1, 8, head), lambda h, iv: (h, 0, 0)),
                pl.BlockSpec((4, rows, 128), lambda h, iv: (0, 0, 0)),
            ],
            scratch_shapes=[pltpu.VMEM((4, rows, head), F32), pltpu.VMEM((4, rows, head), F32)],
        ),
        compiler_params=pltpu.CompilerParams(dimension_semantics=("arbitrary",)),
        name="attn_bwd",
    )(inv, qrot, krot, v, dctx, ctx, lse, qk, qk, rq, rk, gq, gk, cos, sin)


def dqkv_body(inv_width, gq_ref, gk_ref, dv_ref, qk_ref, rq_ref, rk_ref, dq_ref, dk_ref, out_ref):
    width = gq_ref.shape[2]
    for g_ref, r_ref, d_ref, at in (
        (gq_ref, rq_ref, dq_ref, 0),
        (gk_ref, rk_ref, dk_ref, width),
    ):
        rs = r_ref[0]
        hat = qk_ref[0, :, at : at + width] * rs
        value = rs * (g_ref[0] - hat * (d_ref[0] * inv_width))
        out_ref[0, :, at : at + width] = value.astype(BF16)
    out_ref[0, :, 2 * width :] = dv_ref[0]


def dqkv_call(gq, gk, dv, qk, rq, rk, dot_q, dot_k, model):
    _, rows, width = gq.shape
    piece = lambda cols: pl.BlockSpec((1, rows, cols), lambda i: (i, 0, 0))
    return pl.pallas_call(
        functools.partial(dqkv_body, 1.0 / model),
        out_shape=jax.ShapeDtypeStruct((4, rows, 3 * width), BF16),
        grid=(4,),
        in_specs=[piece(width)] * 3 + [piece(2 * width)] + [piece(1)] * 4,
        out_specs=piece(3 * width),
        compiler_params=pltpu.CompilerParams(dimension_semantics=("arbitrary",)),
        name="dqkv",
    )(gq, gk, dv, qk, rq, rk, dot_q, dot_k)


def dinput_body(xord_ref, bidx_ref, d_ref, alo, ahi, blo, bhi, *outs):
    step = pl.program_id(0)
    half = alo.shape[2]

    def write(a_ref, b_ref):
        for i, out in enumerate(outs):
            d = d_ref[i]
            part = dot(d[:, :half], a_ref[0], COLS) + dot(d[:, half:], b_ref[0], COLS)
            out[...] = part.astype(out.dtype)

    @pl.when(step < BLOCKS // 2)
    def _():
        write(alo, blo)

    @pl.when(step >= BLOCKS // 2)
    def _():
        write(ahi, bhi)


def dinput_call(dqkv, weights, xord, bidx, at, dtypes, model):
    _, rows, cols = dqkv.shape
    kb = model // BLOCKS
    half = weights[0].shape[2]
    lo = lambda j, xo, bi: (jnp.minimum(j, BLOCKS // 2 - 1), 0, 0)
    hi = lambda j, xo, bi: (jnp.maximum(j - BLOCKS // 2, 0), 0, 0)
    lob = lambda j, xo, bi: (bi[jnp.minimum(j, BLOCKS // 2 - 1)], 0, 0)
    hib = lambda j, xo, bi: (bi[jnp.maximum(j, BLOCKS // 2)] - BLOCKS // 2, 0, 0)
    return pl.pallas_call(
        dinput_body,
        out_shape=tuple(jax.ShapeDtypeStruct((rows, model), t) for t in dtypes),
        grid_spec=pltpu.PrefetchScalarGridSpec(
            num_scalar_prefetch=2,
            grid=(BLOCKS,),
            in_specs=[
                pl.BlockSpec((2, rows, cols), lambda j, xo, bi: (at, 0, 0)),
                pl.BlockSpec((1, kb, half), lo),
                pl.BlockSpec((1, kb, half), hi),
                pl.BlockSpec((1, kb, half), lob),
                pl.BlockSpec((1, kb, half), hib),
            ],
            out_specs=[pl.BlockSpec((rows, kb), lambda j, xo, bi: (0, xo[j]))] * 2,
        ),
        compiler_params=pltpu.CompilerParams(dimension_semantics=("arbitrary",)),
        name="dinput",
    )(xord, bidx, dqkv, *weights)


def wgrad_body(xord_ref, posa_ref, posb_ref, x0, x1, x2, x3, d_ref, g_ref, a_ref, b_ref):
    kb = x0.shape[1]
    half = b_ref.shape[2]
    for out, lo in ((a_ref, 0), (b_ref, half)):
        total = None
        for i, x in enumerate((x0, x1, x2, x3)):
            part = dot(x[...], d_ref[i, :, lo : lo + half], ROWS)
            total = part if total is None else total + part
        out[0, :kb] = total.astype(BF16)
    a_ref[0, kb:] = g_ref[0]


def wgrad_call(xs, dqkv, gains, xord, posa, posb):
    rows, model = xs[0].shape
    kb = model // BLOCKS
    half = dqkv.shape[2] // 2
    extra = gains.shape[1]
    return pl.pallas_call(
        wgrad_body,
        out_shape=(
            jax.ShapeDtypeStruct((BLOCKS, kb + extra, half), BF16),
            jax.ShapeDtypeStruct((BLOCKS, kb, half), BF16),
        ),
        grid_spec=pltpu.PrefetchScalarGridSpec(
            num_scalar_prefetch=3,
            grid=(BLOCKS,),
            in_specs=[pl.BlockSpec((rows, kb), lambda j, xo, pa, pb: (0, xo[j]))] * 4
            + [
                pl.BlockSpec(dqkv.shape, lambda j, xo, pa, pb: (0, 0, 0)),
                pl.BlockSpec((1, extra, half), lambda j, xo, pa, pb: (xo[j], 0, 0)),
            ],
            out_specs=[
                pl.BlockSpec((1, kb + extra, half), lambda j, xo, pa, pb: (pa[j], 0, 0)),
                pl.BlockSpec((1, kb, half), lambda j, xo, pa, pb: (pb[j], 0, 0)),
            ],
        ),
        compiler_params=pltpu.CompilerParams(dimension_semantics=("arbitrary",)),
        name="wgrad",
    )(xord, posa, posb, *xs, dqkv, gains)


def on_device(
    n_dp,
    tokens,
    w_query,
    w_key,
    w_value,
    w_out,
    w_gate,
    w_up,
    w_down,
    query_gain,
    key_gain,
    attn_gain,
    mlp_gain,
    cotangent,
):
    fast = n_dp == BLOCKS
    rows, model = tokens.shape
    length = 4 * rows
    heads, gain_part = query_gain.shape
    head = gain_part * n_dp
    width = heads * head
    half = 3 * width // 2
    t = lax.axis_index("tensor")
    d = lax.axis_index("dp")

    third = jnp.where(t < 2, 2, 1)
    fourth = jnp.where(t < 2, 3, 0)
    sid = jnp.stack([t, t ^ 1, third, fourth]).astype(jnp.int32)
    slots = jnp.arange(4, dtype=jnp.int32)
    inv = jnp.sum(jnp.where(sid[None, :] == slots[:, None], slots[None, :], 0), axis=1)
    inv = inv.astype(jnp.int32)

    small = [query_gain.reshape(-1), key_gain.reshape(-1), attn_gain, mlp_gain]
    sizes = [s.shape[0] for s in small]
    extra = 16
    flat = jnp.concatenate(small)
    row = jnp.pad(flat[None, :], ((0, extra - 1), (0, half - flat.shape[0])))
    packed = jnp.concatenate([w_query, w_key, w_value], axis=1)
    pack_a = jnp.concatenate([packed[:, :half], row], axis=0)
    pack_b = packed[:, half:]
    if fast:
        xord = d.astype(jnp.int32) ^ jnp.array(ORDER_A, jnp.int32)
        bidx = jnp.array(SWAP_B, jnp.int32)
        a1 = jnp.stack([pack_a, flip(pack_a, BIT_X)])
        b1 = jnp.stack([pack_b, flip(pack_b, BIT_Y)])
        a2 = jnp.concatenate([a1, flip(a1, BIT_Y)])
        b2 = jnp.concatenate([b1, flip(b1, BIT_X)])
        a3 = flip(a2, BIT_CORE)
        b3 = flip(b2, BIT_CORE)
        weights = (a2, a3, b2, b3)
        rel = jnp.concatenate([a2[:, -extra], a3[:, -extra]])
        place = jnp.zeros((BLOCKS,), jnp.int32).at[xord].set(jnp.arange(BLOCKS, dtype=jnp.int32))
        gains = jnp.take(rel, place, axis=0)
    else:
        xord = jnp.arange(BLOCKS, dtype=jnp.int32)
        bidx = xord
        all_a = lax.all_gather(pack_a, "dp", axis=0)
        all_b = lax.all_gather(pack_b, "dp", axis=0)
        wide_a = all_a[:, :-extra].reshape(BLOCKS, -1, half)
        wide_b = all_b.reshape(BLOCKS, -1, half)
        weights = (wide_a[:4], wide_a[4:], wide_b[:4], wide_b[4:])
        gains = all_a[:, -extra]
    at = [sum(sizes[:i]) for i in range(5)]

    def head_gain(values):
        values = values.reshape(n_dp, heads, gain_part).transpose(1, 0, 2)
        return values.reshape(heads, 1, head).astype(F32)

    gain_q = head_gain(gains[:, at[0] : at[1]])
    gain_k = head_gain(gains[:, at[1] : at[2]])
    gain_attn = gains[:, at[2] : at[3]].reshape(1, model).astype(F32)
    gain_mlp = gains[:, at[3] : at[4]].reshape(1, model).astype(F32)

    full_out = lax.all_gather(w_out, "dp", axis=1, tiled=True)
    full_gate = lax.all_gather(w_gate, "dp", axis=0, tiled=True)
    full_up = lax.all_gather(w_up, "dp", axis=0, tiled=True)
    full_down = lax.all_gather(w_down, "dp", axis=1, tiled=True)

    cos, sin = rope_tables(length, head)

    xs = line_gather(tokens)
    prev = qkv_call(xs[:2], weights, xord, bidx, 0, None, width)
    prev = qkv_call(xs[2:3], weights, xord, bidx, 2, prev, width)
    qk, v, squares = qkv_call(xs[3:], weights, xord, bidx, 3, prev, width)
    sums = jnp.take(squares[:, :, :2].transpose(0, 2, 1), inv, axis=0)
    sums = jnp.take(lax.psum(sums, "tensor"), sid, axis=0)
    rs = lax.rsqrt(sums / model + norm_eps)[..., None]
    rq, rk = rs[:, 0], rs[:, 1]
    qrot, krot, ctx, lse = attn_fwd(inv, qk, v, rq, rk, gain_q, gain_k, cos, sin)

    def out_part(i, out=BF16):
        return dot(ctx[i], full_out, out=out)

    p3, p2, p1, p0 = out_part(3), out_part(2), out_part(1), out_part(0, F32)
    attn_part = line_scatter(p0, p1, p2, p3)
    attn_rs = lax.rsqrt(jnp.mean(attn_part * attn_part, axis=1, keepdims=True) + norm_eps)
    attn_hat = attn_part * attn_rs
    residual = tokens.astype(F32) + attn_hat * gain_attn

    mids = line_gather(residual.astype(BF16))
    gates, ups, hiddens, parts = [], [], [], []
    for i in range(4):
        gate = dot(mids[i], full_gate)
        up = dot(mids[i], full_up)
        hidden = (gate * jax.nn.sigmoid(gate) * up).astype(BF16)
        parts.append(dot(hidden, full_down, out=F32 if i == 0 else BF16))
        gates.append(gate)
        ups.append(up)
        hiddens.append(hidden)
    mlp_part = line_scatter(*parts)
    mlp_rs = lax.rsqrt(jnp.mean(mlp_part * mlp_part, axis=1, keepdims=True) + norm_eps)
    mlp_hat = mlp_part * mlp_rs
    layer_output = (residual + mlp_hat * gain_mlp).astype(BF16)
    upstream = cotangent.astype(F32)
    mlp_gain_part = jnp.sum(upstream * mlp_hat, axis=0)
    d_mlp_norm = upstream * gain_mlp
    d_mlp = mlp_rs * (d_mlp_norm - mlp_hat * jnp.mean(d_mlp_norm * mlp_hat, axis=1, keepdims=True))

    dms = line_gather(d_mlp.astype(BF16))
    d_gates, d_ups, parts = [], [], []
    for i in range(4):
        gate, up = gates[i], ups[i]
        d_hidden = dot(dms[i], full_down, COLS)
        sig = jax.nn.sigmoid(gate)
        d_up = (d_hidden * gate * sig).astype(BF16)
        d_gate = (d_hidden * up * sig * (1.0 + gate * (1.0 - sig))).astype(BF16)
        part = dot(d_gate, full_gate, COLS) + dot(d_up, full_up, COLS)
        parts.append(part if i == 0 else part.astype(BF16))
        d_gates.append(d_gate)
        d_ups.append(d_up)
    d_residual = upstream + line_scatter(*parts)
    dm_all = jnp.concatenate(dms)
    mid_all = jnp.concatenate(mids)
    grad_down = dot(jnp.concatenate(hiddens), dm_all, ROWS, BF16)
    grad_gate = dot(mid_all, jnp.concatenate(d_gates), ROWS, BF16)
    grad_up = dot(mid_all, jnp.concatenate(d_ups), ROWS, BF16)
    grad_gate, grad_up, grad_down = (
        lax.psum_scatter(grad_gate, "dp", scatter_dimension=0, tiled=True).astype(F32),
        lax.psum_scatter(grad_up, "dp", scatter_dimension=0, tiled=True).astype(F32),
        lax.psum_scatter(grad_down, "dp", scatter_dimension=1, tiled=True).astype(F32),
    )

    attn_gain_part = jnp.sum(d_residual * attn_hat, axis=0)
    d_attn_norm = d_residual * gain_attn
    d_attn = attn_rs * (
        d_attn_norm - attn_hat * jnp.mean(d_attn_norm * attn_hat, axis=1, keepdims=True)
    )

    das = line_gather(d_attn.astype(BF16))
    dctx = jnp.stack([dot(das[i], full_out, COLS, BF16) for i in range(4)])
    grad_out = dot(ctx.reshape(length, width), jnp.concatenate(das), ROWS, BF16)
    grad_out = lax.psum_scatter(grad_out, "dp", scatter_dimension=1, tiled=True).astype(F32)
    gq, gk, dv, head_gains, dots = attn_bwd(
        inv, qrot, krot, v, dctx, ctx, lse, qk, rq, rk, gain_q, gain_k, cos, sin
    )
    dots = jnp.take(dots[:, :, :2].transpose(0, 2, 1), inv, axis=0)
    dots, attn_gain_sum, mlp_gain_sum = lax.psum((dots, attn_gain_part, mlp_gain_part), "tensor")
    dots = jnp.take(dots, sid, axis=0)[..., None]
    dqkv = dqkv_call(gq, gk, dv, qk, rq, rk, dots[:, 0], dots[:, 1], model)
    p2, p3 = dinput_call(dqkv, weights, xord, bidx, 1, (BF16, BF16), model)
    p0, p1 = dinput_call(dqkv, weights, xord, bidx, 0, (F32, BF16), model)
    grad_tokens = d_residual + line_scatter(p0, p1, p2, p3)

    def spread(values):
        values = values.reshape(heads, n_dp, gain_part).transpose(1, 0, 2)
        return values.reshape(n_dp, heads * gain_part)

    gain_rows = jnp.concatenate(
        [
            spread(head_gains[:, 0]),
            spread(head_gains[:, 1]),
            attn_gain_sum.reshape(n_dp, -1),
            mlp_gain_sum.reshape(n_dp, -1),
        ],
        axis=1,
    )
    gain_rows = jnp.pad(gain_rows, ((0, 0), (0, half - gain_rows.shape[1])))
    if fast:
        packed_gains = jnp.pad(gain_rows[:, None, :], ((0, 0), (0, extra - 1), (0, 0)))
        spot_a = {p: j for j, p in enumerate((0, 4, 2, 6, 1, 5, 3, 7))}
        spot_b = {p: j for j, p in enumerate((0, 2, 4, 6, 1, 3, 5, 7))}
        posa = jnp.array([spot_a[p] for p in ORDER_A], jnp.int32)
        posb = jnp.array([spot_b[p] for p in ORDER_A], jnp.int32)
        g_a, g_b = wgrad_call(xs, dqkv, packed_gains.astype(BF16), xord, posa, posb)
        for bits in ((BIT_CORE, BIT_CORE), (BIT_X, BIT_Y), (BIT_Y, BIT_X)):
            n = g_a.shape[0] // 2
            g_a = g_a[:n] + flip(g_a[n:], bits[0])
            g_b = g_b[:n] + flip(g_b[n:], bits[1])
        g_a, g_b = g_a[0], g_b[0]
        gain_row = g_a[-extra].astype(F32)
        g_a = g_a[:-extra]
    else:
        spots = jnp.arange(BLOCKS, dtype=jnp.int32)
        packed_gains = jnp.zeros((BLOCKS, extra, half), BF16)
        g_a, g_b = wgrad_call(xs, dqkv, packed_gains, xord, spots, spots)
        g_a = g_a[:, :-extra].reshape(model, half)
        g_b = g_b.reshape(model, half)
        g_a = lax.psum_scatter(g_a, "dp", scatter_dimension=0, tiled=True)
        g_b = lax.psum_scatter(g_b, "dp", scatter_dimension=0, tiled=True)
        gain_row = lax.psum_scatter(gain_rows, "dp", scatter_dimension=0, tiled=True)[0]
    grad_qkv = jnp.concatenate([g_a, g_b], axis=1).astype(F32)
    return (
        layer_output,
        grad_tokens,
        grad_qkv[:, :width],
        grad_qkv[:, width : 2 * width],
        grad_qkv[:, 2 * width :],
        grad_out,
        grad_gate,
        grad_up,
        grad_down,
        gain_row[at[0] : at[1]].reshape(heads, gain_part),
        gain_row[at[1] : at[2]].reshape(heads, gain_part),
        gain_row[at[2] : at[3]],
        gain_row[at[3] : at[4]],
    )


def solution(mesh):
    in_specs = (
        P(("dp", "tensor"), None),
        P("dp", "tensor"),
        P("dp", "tensor"),
        P("dp", "tensor"),
        P("tensor", "dp"),
        P("dp", "tensor"),
        P("dp", "tensor"),
        P("tensor", "dp"),
        P("tensor", "dp"),
        P("tensor", "dp"),
        P("dp"),
        P("dp"),
        P(("dp", "tensor"), None),
    )
    out_specs = (
        P(("dp", "tensor"), None),
        P(("dp", "tensor"), None),
        P("dp", "tensor"),
        P("dp", "tensor"),
        P("dp", "tensor"),
        P("tensor", "dp"),
        P("dp", "tensor"),
        P("dp", "tensor"),
        P("tensor", "dp"),
        P("tensor", "dp"),
        P("tensor", "dp"),
        P("dp"),
        P("dp"),
    )
    assert mesh.shape["tensor"] == 4
    return jax.shard_map(
        functools.partial(on_device, mesh.shape["dp"]),
        mesh=mesh,
        in_specs=in_specs,
        out_specs=out_specs,
        check_vma=False,
    )
```

```python
import functools
import math

import jax
import jax.numpy as jnp
from jax import lax
from jax.experimental import pallas as pl
from jax.experimental.pallas import tpu as pltpu
from jax.sharding import PartitionSpec as P


rope_theta = 500000.0
norm_eps = 1e-06

F32 = jnp.float32
BF16 = jnp.bfloat16

PAIRS = [(0, 1), (1, 0), (2, 3), (3, 2)]
MIDDLE = [(1, 2), (2, 1)]
OUTWARD = [(2, 3), (1, 0)]
INWARD = [(3, 2), (0, 1)]

ORDER = (0, 2, 4, 6, 1, 3, 5, 7)
BLOCKS = 8
BIT_CORE, BIT_X, BIT_Y = 1, 2, 4
CHUNKS = 2
NCOL = 512

COLS = ((1,), (1,))
ROWS = ((0,), (0,))


def rope_tables(length, head_size):
    half_size = head_size // 2
    freqs = rope_theta ** (-(jnp.arange(half_size, dtype=F32) * 2.0) / head_size)
    angles = jnp.arange(length, dtype=F32)[:, None] * freqs[None, :]
    cosine, sine = jnp.cos(angles), jnp.sin(angles)
    return (
        jnp.concatenate([cosine, cosine], axis=1),
        jnp.concatenate([-sine, sine], axis=1),
    )


def shift(value, pairs):
    return lax.ppermute(value, "tensor", pairs)


def line_gather(own):
    e1 = shift(own, PAIRS)
    m_own = shift(own, MIDDLE)
    m_e1 = shift(e1, MIDDLE)
    f_own = shift(m_own, OUTWARD)
    f_e1 = shift(m_e1, OUTWARD)
    return own, e1, m_own, f_own, m_e1, f_e1


def line_scatter(parts):
    own, p1, p2, p3 = parts
    b3 = shift(p3, INWARD)
    b2 = shift(p2, INWARD)
    s3 = p3 + b3
    m3 = shift(s3, MIDDLE)
    s2 = p2 + b2
    m2 = shift(s2, MIDDLE)
    s1 = p1 + m3
    e1 = shift(s1, PAIRS)
    return own, e1, m2


def everyone(value):
    return [shift(value, [(i, (i + k) % 4) for i in range(4)]) for k in (1, 2, 3)]


def flip(value, bit):
    return lax.ppermute(value, "dp", [(i, i ^ bit) for i in range(8)])


def dot(a, b, dims=((1,), (0,)), out=F32):
    return lax.dot_general(a, b, (dims, ((), ())), preferred_element_type=F32).astype(out)


def call(body, *args, grid, in_specs, out_specs, out_shape, flops, prefetch=0, **kw):
    size = sum(math.prod(a.shape) * a.dtype.itemsize for a in args)
    size += sum(math.prod(s.shape) * s.dtype.itemsize for s in out_shape)
    return pl.pallas_call(
        body,
        out_shape=out_shape,
        grid_spec=pltpu.PrefetchScalarGridSpec(
            num_scalar_prefetch=prefetch,
            grid=grid,
            in_specs=in_specs,
            out_specs=out_specs,
            scratch_shapes=kw.pop("scratch", []),
        ),
        input_output_aliases=kw.pop("alias", {}),
        compiler_params=pltpu.CompilerParams(
            dimension_semantics=("arbitrary",) * len(grid)
        ),
        cost_estimate=pl.CostEstimate(
            flops=int(flops), transcendentals=0, bytes_accessed=int(size)
        ),
    )(*args)


ANY = pl.BlockSpec(memory_space=pl.ANY)


def whole(shape):
    return pl.BlockSpec(shape, lambda *_: (0,) * len(shape))


def spec(shape, *at):
    return pl.BlockSpec(shape, lambda j, *_: tuple(j if a is None else a for a in at))


def struct(shape, dtype):
    return jax.ShapeDtypeStruct(shape, dtype)


def chain(prev, at, shapes):
    if prev is None:
        return [], [], {}
    return list(prev), [ANY] * len(prev), {at + i: o for i, o in enumerate(shapes)}


def load_pieces(refs, store):
    own, e1, m_own, f_own, m_e1, f_e1 = refs
    store(0, own[...])
    store(1, e1[...])
    store(2, m_own[...] + f_own[...])
    store(3, m_e1[...] + f_e1[...])


def qkv_body(x_at, has_prev, sid_ref, xord_ref, *refs):
    pieces = refs[:6]
    alo, ahi, blo, bhi = refs[6:10]
    refs = refs[10:]
    if has_prev:
        prev_sums = refs[0]
        refs = refs[4:]
    qk_ref, v_ref, x_ref, sums_ref, xs, sq = refs
    step = pl.program_id(0)
    rows, model = pieces[0].shape
    kb = model // BLOCKS
    cols = alo.shape[2]

    @pl.when(step == 0)
    def _():
        def store(i, value):
            x_ref[0, i * rows : (i + 1) * rows] = value

        load_pieces(pieces, store)
        for j in range(BLOCKS):
            at = pl.multiple_of(xord_ref[j] * kb, kb)
            xs[:, j * kb : (j + 1) * kb] = x_ref[0, :, pl.ds(at, kb)]
        sq[...] = jnp.zeros_like(sq)

    def work(lo_ref, hi_ref):
        low = lo_ref[...].reshape(4 * kb, cols)
        high = hi_ref[...].reshape(4 * kb, cols)
        value = dot(xs[:, : 4 * kb], low) + dot(xs[:, 4 * kb :], high)

        @pl.when(step < 4)
        def _():
            qk_ref[...] = value.reshape(qk_ref.shape)
            lane = lax.broadcasted_iota(jnp.int32, sq.shape, 1)
            row = jnp.sum(value * value, axis=1, keepdims=True)
            sq[...] += jnp.where(lane == step // 2, row, 0.0)

        @pl.when(step >= 4)
        def _():
            v_ref[...] = value.astype(BF16).reshape(v_ref.shape)

    @pl.when(step < 3)
    def _():
        work(alo, ahi)

    @pl.when(step >= 3)
    def _():
        work(blo, bhi)

    @pl.when(step == 5)
    def _():
        if has_prev:
            sums_ref[...] = prev_sums[...]
        else:
            sums_ref[...] = jnp.zeros_like(sums_ref)
        for i in range(4):
            flipped = sq[i * rows : (i + 1) * rows, :].T
            at = pl.multiple_of(sid_ref[i] * rows, rows)
            sums_ref[8 * x_at : 8 * x_at + 8, pl.ds(at, rows)] = flipped[:8]


def qkv_call(x, pieces, weights, sid, xord, prev, width):
    rows, model = pieces[0].shape
    kb = model // BLOCKS
    cols = width // 2
    shapes = (
        struct((4, CHUNKS * rows, 2 * width), F32),
        struct((4, CHUNKS * rows, width), BF16),
        struct((CHUNKS, 4 * rows, model), BF16),
        struct((8 * CHUNKS, 4 * rows), F32),
    )
    extra, extra_specs, alias = [], [], {}
    if prev is not None:
        extra = [prev[3], *prev[:3]]
        extra_specs = [whole(shapes[3].shape), ANY, ANY, ANY]
        alias = {13 + i: i for i in range(3)}
    weight = lambda at: pl.BlockSpec((4, kb, cols), lambda j, *_: (0, 0, at(j)))
    return call(
        functools.partial(qkv_body, x, prev is not None),
        sid,
        xord,
        *pieces,
        *weights,
        *extra,
        grid=(6,),
        prefetch=2,
        in_specs=[whole((rows, model))] * 6
        + [weight(lambda j: jnp.minimum(j, 2))] * 2
        + [weight(lambda j: jnp.maximum(j - 3, 0))] * 2
        + extra_specs,
        out_specs=[
            pl.BlockSpec((4, rows, cols), lambda j, *_: (0, x, jnp.minimum(j, 3))),
            pl.BlockSpec((4, rows, cols), lambda j, *_: (0, x, jnp.maximum(j - 4, 0))),
            spec((1, 4 * rows, model), x, 0, 0),
            whole(shapes[3].shape),
        ],
        out_shape=shapes,
        alias=alias,
        scratch=[pltpu.VMEM((4 * rows, model), BF16), pltpu.VMEM((4 * rows, 128), F32)],
        flops=2 * 4 * rows * model * 3 * width,
    )


def out_body(ctx_ref, w_ref, p0, p1, p2, p3):
    rows = ctx_ref.shape[1]
    value = dot(ctx_ref[...].reshape(4 * rows, -1), w_ref[...])
    for i, out in enumerate((p0, p1, p2, p3)):
        out[...] = value[i * rows : (i + 1) * rows].astype(out.dtype)


def out_call(x, ctx, w_out):
    _, all_rows, width = ctx.shape
    rows = all_rows // CHUNKS
    model = w_out.shape[1]
    return call(
        out_body,
        ctx,
        w_out,
        grid=(model // NCOL,),
        in_specs=[spec((4, rows, width), 0, x, 0), spec((width, NCOL), 0, None)],
        out_specs=[spec((rows, NCOL), 0, None)] * 4,
        out_shape=[struct((rows, model), t) for t in (F32, BF16, BF16, BF16)],
        flops=2 * 4 * rows * width * model,
    )


def dctx_body(*refs):
    pieces, w_ref, (ctx_ref, da_ref) = refs[:6], refs[6], refs[-2:]
    rows = pieces[0].shape[0]

    def store(i, value):
        da_ref[0, i * rows : (i + 1) * rows] = value

    load_pieces(pieces, store)
    ctx_ref[...] = dot(da_ref[0], w_ref[...], COLS, BF16).reshape(ctx_ref.shape)


def dctx_call(x, pieces, w_out, prev):
    rows, model = pieces[0].shape
    width = w_out.shape[0]
    extra, extra_specs, alias = chain(prev, 7, (0, 1))
    return call(
        dctx_body,
        *pieces,
        w_out,
        *extra,
        grid=(1,),
        in_specs=[whole((rows, model))] * 6 + [whole((width, model))] + extra_specs,
        out_specs=[spec((4, rows, width), 0, x, 0), spec((1, 4 * rows, model), x, 0, 0)],
        out_shape=[
            struct((4, CHUNKS * rows, width), BF16),
            struct((CHUNKS, 4 * rows, model), BF16),
        ],
        alias=alias,
        flops=2 * 4 * rows * width * model,
    )


def gout_body(ctx_ref, da_ref, out_ref, flipped):
    rows = ctx_ref.shape[1] // CHUNKS

    @pl.when(pl.program_id(0) == 0)
    def _():
        for x in range(CHUNKS):
            for i in range(4):
                at = (4 * x + i) * rows
                flipped[:, at : at + rows] = ctx_ref[i, x * rows : (x + 1) * rows].T

    out_ref[...] = dot(flipped[...], da_ref[...].reshape(8 * rows, -1), out=BF16)


def gout_call(ctx, das):
    _, all_rows, width = ctx.shape
    model = das.shape[2]
    return call(
        gout_body,
        ctx,
        das,
        grid=(model // NCOL,),
        in_specs=[whole(ctx.shape), spec((*das.shape[:2], NCOL), 0, 0, None)],
        out_specs=[spec((width, NCOL), 0, None)],
        out_shape=[struct((width, model), BF16)],
        scratch=[pltpu.VMEM((width, 4 * all_rows), BF16)],
        flops=2 * 4 * all_rows * width * model,
    )[0]


def column(row):
    return jnp.broadcast_to(row, (128, row.shape[1])).T


def attn_fwd_body(
    scale,
    inv_model,
    inv_ref,
    q_ref,
    k_ref,
    v_ref,
    s0,
    s1,
    s2,
    s3,
    gq_ref,
    gk_ref,
    cos_ref,
    sin_ref,
    qrot_ref,
    krot_ref,
    ctx_ref,
    lse_ref,
    rq_ref,
    rk_ref,
):
    rows, head = q_ref.shape[1:]
    part = rows // CHUNKS
    gq, gk = gq_ref[0], gk_ref[0]

    @pl.when(pl.program_id(0) == 0)
    def _():
        rs = lax.rsqrt((s0[...] + s1[...] + s2[...] + s3[...]) * inv_model + norm_eps)
        for b in range(4):
            r = inv_ref[b]
            for x in range(CHUNKS):
                for out, at in ((rq_ref, 8 * x), (rk_ref, 8 * x + 1)):
                    out[r, x * part : (x + 1) * part] = column(
                        rs[at : at + 1, b * part : (b + 1) * part]
                    )

    for b in range(4):
        r = inv_ref[b]
        cos = cos_ref[b * rows : (b + 1) * rows]
        sin = sin_ref[b * rows : (b + 1) * rows]
        qn = q_ref[r] * rq_ref[r] * gq
        kn = k_ref[r] * rk_ref[r] * gk
        qrot_ref[r] = (qn * cos + pltpu.roll(qn, head // 2, 1) * sin).astype(BF16)
        krot_ref[r] = (kn * cos + pltpu.roll(kn, head // 2, 1) * sin).astype(BF16)
    causal = lax.broadcasted_iota(jnp.int32, (rows, rows), 0) >= lax.broadcasted_iota(
        jnp.int32, (rows, rows), 1
    )
    for b in range(4):
        r = inv_ref[b]
        q = qrot_ref[r]
        parts = []
        for c in range(b + 1):
            s = dot(q, krot_ref[inv_ref[c]], COLS) * scale
            if c == b:
                s = jnp.where(causal, s, -1e30)
            parts.append(s)
        top = jnp.max(parts[0], axis=1, keepdims=True)
        for s in parts[1:]:
            top = jnp.maximum(top, jnp.max(s, axis=1, keepdims=True))
        exps = [jnp.exp(s - top) for s in parts]
        total = jnp.sum(exps[0], axis=1, keepdims=True)
        for e in exps[1:]:
            total = total + jnp.sum(e, axis=1, keepdims=True)
        inverse = 1.0 / total
        ctx = None
        for c in range(b + 1):
            piece = dot((exps[c] * inverse).astype(BF16), v_ref[inv_ref[c]])
            ctx = piece if ctx is None else ctx + piece
        ctx_ref[r] = ctx.astype(BF16)
        lse_ref[0, r] = top + jnp.log(total)


def attn_fwd(inv, qk, v, sums, gq, gk, cos, sin, model):
    _, rows, width2 = qk.shape
    width = width2 // 2
    heads, _, head = gq.shape
    per_head = spec((4, rows, head), 0, 0, None)
    return call(
        functools.partial(attn_fwd_body, 1.0 / math.sqrt(head), 1.0 / model),
        inv,
        qk,
        qk,
        v,
        *sums,
        gq,
        gk,
        cos,
        sin,
        grid=(heads,),
        prefetch=1,
        in_specs=[
            per_head,
            pl.BlockSpec((4, rows, head), lambda h, iv: (0, 0, heads + h)),
            per_head,
        ]
        + [whole(sums[0].shape)] * 4
        + [spec((1, 1, head), None, 0, 0)] * 2
        + [whole(cos.shape)] * 2,
        out_specs=[per_head] * 3
        + [spec((1, 4, rows, 1), None, 0, 0, 0)]
        + [whole((4, rows, 128))] * 2,
        out_shape=[struct((4, rows, width), BF16)] * 3
        + [struct((heads, 4, rows, 1), F32)]
        + [struct((4, rows, 128), F32)] * 2,
        flops=4e9,
    )


def attn_bwd_body(
    scale,
    inv_ref,
    qrot_ref,
    krot_ref,
    v_ref,
    dctx_ref,
    ctx_ref,
    lse_ref,
    q_ref,
    k_ref,
    rq_ref,
    rk_ref,
    gq_ref,
    gk_ref,
    cos_ref,
    sin_ref,
    extra_ref,
    dq_ref,
    dk_ref,
    dv_ref,
    gain_ref,
    dots_ref,
    dk_acc,
    dv_acc,
    dots,
):
    rows, head = q_ref.shape[1:]
    part = rows // CHUNKS
    causal = lax.broadcasted_iota(jnp.int32, (rows, rows), 0) >= lax.broadcasted_iota(
        jnp.int32, (rows, rows), 1
    )
    lane = lax.broadcasted_iota(jnp.int32, (rows, 128), 1)
    gq, gk = gq_ref[0], gk_ref[0]
    first = pl.program_id(0) == 0

    def finish(raw, b, r, raw_ref, rs_ref, gain, out_ref):
        cos = cos_ref[b * rows : (b + 1) * rows]
        sin = sin_ref[b * rows : (b + 1) * rows]
        norm = raw * cos - pltpu.roll(raw, head // 2, 1) * sin
        hat = raw_ref[r] * rs_ref[r]
        both = norm * hat
        out_ref[r] = norm * gain
        return (
            jnp.sum(both, axis=0, keepdims=True),
            jnp.sum(both * gain, axis=1, keepdims=True),
        )

    q_gain = jnp.zeros((1, head), F32)
    k_gain = jnp.zeros((1, head), F32)
    q_dots = []
    for b in range(4):
        r = inv_ref[b]
        q = qrot_ref[r]
        dctx = dctx_ref[r]
        lse = lse_ref[0, r]
        delta = jnp.sum(dctx.astype(F32) * ctx_ref[r].astype(F32), axis=1, keepdims=True)
        dq = None
        for c in range(b + 1):
            rc = inv_ref[c]
            k = krot_ref[rc]
            s = dot(q, k, COLS) * scale
            if c == b:
                s = jnp.where(causal, s, -1e30)
            p = jnp.exp(s - lse)
            dp = dot(dctx, v_ref[rc], COLS)
            ds = (p * (dp - delta) * scale).astype(BF16)
            dv_part = dot(p.astype(BF16), dctx, ROWS)
            dk_part = dot(ds, q, ROWS)
            dq_part = dot(ds, k)
            dq = dq_part if dq is None else dq + dq_part
            if c == b:
                dv_acc[c] = dv_part
                dk_acc[c] = dk_part
            else:
                dv_acc[c] += dv_part
                dk_acc[c] += dk_part
        gain_part, row_dot = finish(dq, b, r, q_ref, rq_ref, gq, dq_ref)
        q_gain = q_gain + gain_part
        q_dots.append(row_dot)
    for b in range(4):
        r = inv_ref[b]
        gain_part, row_dot = finish(dk_acc[b], b, r, k_ref, rk_ref, gk, dk_ref)
        k_gain = k_gain + gain_part
        dv_ref[r] = dv_acc[b].astype(BF16)
        old = jnp.where(first, 0.0, dots[b])
        dots[b] = old + jnp.where(lane == 0, q_dots[b], jnp.where(lane == 1, row_dot, 0.0))
    row = lax.broadcasted_iota(jnp.int32, (8, head), 0)
    gain_ref[0] = jnp.where(row == 0, q_gain, jnp.where(row == 1, k_gain, 0.0))

    @pl.when(pl.program_id(0) == pl.num_programs(0) - 1)
    def _():
        for b in range(4):
            for x in range(CHUNKS):
                flipped = dots[b, x * part : (x + 1) * part].T
                dots_ref[8 * x : 8 * x + 8, b * part : (b + 1) * part] = flipped[:8]
        dots_ref[8 * CHUNKS :] = extra_ref[...]


def attn_bwd(inv, qrot, krot, v, dctx, ctx, lse, qk, rq, rk, gq, gk, cos, sin, extra):
    _, rows, width = qrot.shape
    heads, _, head = gq.shape
    per_head = spec((4, rows, head), 0, 0, None)
    dots_shape = (8 * CHUNKS + extra.shape[0], extra.shape[1])
    return call(
        functools.partial(attn_bwd_body, 1.0 / math.sqrt(head)),
        inv,
        qrot,
        krot,
        v,
        dctx,
        ctx,
        lse,
        qk,
        qk,
        rq,
        rk,
        gq,
        gk,
        cos,
        sin,
        extra,
        grid=(heads,),
        prefetch=1,
        in_specs=[per_head] * 5
        + [
            spec((1, 4, rows, 1), None, 0, 0, 0),
            per_head,
            pl.BlockSpec((4, rows, head), lambda h, iv: (0, 0, heads + h)),
        ]
        + [whole((4, rows, 128))] * 2
        + [spec((1, 1, head), None, 0, 0)] * 2
        + [whole(cos.shape)] * 2
        + [whole(extra.shape)],
        out_specs=[per_head] * 3
        + [spec((1, 8, head), None, 0, 0)]
        + [whole(dots_shape)],
        out_shape=[struct((4, rows, width), F32)] * 2
        + [
            struct((4, rows, width), BF16),
            struct((heads, 8, head), F32),
            struct(dots_shape, F32),
        ],
        scratch=[pltpu.VMEM((4, rows, head), F32)] * 2 + [pltpu.VMEM((4, rows, 128), F32)],
        flops=12e9,
    )


def dinput_body(x_at, inv_model, sid_ref, xord_ref, *refs):
    d0, d1, d2, d3, gq_ref, gk_ref, dv_ref, qk_ref, rq_ref, rk_ref = refs[:10]
    alo, ahi, blo, bhi = refs[10:14]
    p0, p1, p2, p3, out_ref = refs[-5:]
    step = pl.program_id(0)
    rows, width = gq_ref.shape[1:]
    kb = alo.shape[1]
    half = alo.shape[2]

    @pl.when(step == 0)
    def _():
        total = (d0[...] + d1[...] + d2[...] + d3[...]) * inv_model
        for i in range(4):
            for g_ref, r_ref, row, at in (
                (gq_ref, rq_ref, 8 * x_at, 0),
                (gk_ref, rk_ref, 8 * x_at + 1, width),
            ):
                rs = r_ref[i]
                sums = jnp.zeros((1, rows), F32)
                for b in range(4):
                    here = total[row : row + 1, b * rows : (b + 1) * rows]
                    sums = jnp.where(sid_ref[i] == b, here, sums)
                mean = column(sums)
                for h in range(width // 128):
                    lo = at + h * 128
                    hat = qk_ref[i, :, lo : lo + 128] * rs
                    value = rs * (g_ref[i, :, h * 128 : (h + 1) * 128] - hat * mean)
                    out_ref[0, i * rows : (i + 1) * rows, lo : lo + 128] = value.astype(BF16)
            out_ref[0, i * rows : (i + 1) * rows, 2 * width :] = dv_ref[i]

    def work(a_ref, b_ref):
        for q in range(2):
            value = dot(out_ref[0, :, :half], a_ref[q], COLS) + dot(
                out_ref[0, :, half:], b_ref[q], COLS
            )
            at = pl.multiple_of(xord_ref[2 * step + q] * kb, kb)
            for i, out in enumerate((p0, p1, p2, p3)):
                out[:, pl.ds(at, kb)] = value[i * rows : (i + 1) * rows].astype(out.dtype)

    @pl.when(step < 2)
    def _():
        work(alo, blo)

    @pl.when(step >= 2)
    def _():
        work(ahi, bhi)


def dinput_call(x, dots, gq, gk, dv, qk, rq, rk, weights, sid, xord, prev, model):
    _, all_rows, width = gq.shape
    rows = all_rows // CHUNKS
    kb = model // BLOCKS
    half = weights[0].shape[2]
    part = lambda cols: spec((4, rows, cols), 0, x, 0)
    low = pl.BlockSpec((2, kb, half), lambda j, *_: (jnp.minimum(j, 1), 0, 0))
    high = pl.BlockSpec((2, kb, half), lambda j, *_: (jnp.maximum(j - 2, 0), 0, 0))
    extra, extra_specs, alias = chain(prev, 16, (4,))
    return call(
        functools.partial(dinput_body, x, 1.0 / model),
        sid,
        xord,
        *dots,
        gq,
        gk,
        dv,
        qk,
        rq,
        rk,
        *weights,
        *extra,
        grid=(4,),
        prefetch=2,
        in_specs=[whole(dots[0].shape)] * 4
        + [part(width)] * 3
        + [part(2 * width)]
        + [part(128)] * 2
        + [low, high, low, high]
        + extra_specs,
        out_specs=[whole((rows, model))] * 4 + [spec((1, 4 * rows, 3 * width), x, 0, 0)],
        out_shape=[struct((rows, model), t) for t in (F32, BF16, BF16, BF16)]
        + [struct((CHUNKS, 4 * rows, 3 * width), BF16)],
        alias=alias,
        flops=2 * 4 * rows * model * 3 * width,
    )


def wgrad_body(xord_ref, posa_ref, posb_ref, x_ref, d_ref, g_ref, a_ref, b_ref):
    kb = x_ref.shape[2]
    half = b_ref.shape[2]
    flipped = [x_ref[x].T for x in range(CHUNKS)]
    for out, lo in ((a_ref, 0), (b_ref, half)):
        total = None
        for x in range(CHUNKS):
            part = dot(flipped[x], d_ref[x, :, lo : lo + half])
            total = part if total is None else total + part
        out[0, :kb] = total.astype(BF16)
    a_ref[0, kb:] = g_ref[0]


def wgrad_call(xs, dqkv, gains, xord, posa, posb):
    _, tall, model = xs.shape
    kb = model // BLOCKS
    half = dqkv.shape[2] // 2
    extra = gains.shape[1]
    return call(
        wgrad_body,
        xord,
        posa,
        posb,
        xs,
        dqkv,
        gains,
        grid=(BLOCKS,),
        prefetch=3,
        in_specs=[
            pl.BlockSpec((CHUNKS, tall, kb), lambda j, xo, pa, pb: (0, 0, xo[j])),
            whole(dqkv.shape),
            pl.BlockSpec((1, extra, half), lambda j, xo, pa, pb: (xo[j], 0, 0)),
        ],
        out_specs=[
            pl.BlockSpec((1, kb + extra, half), lambda j, xo, pa, pb: (pa[j], 0, 0)),
            pl.BlockSpec((1, kb, half), lambda j, xo, pa, pb: (pb[j], 0, 0)),
        ],
        out_shape=[
            struct((BLOCKS, kb + extra, half), BF16),
            struct((BLOCKS, kb, half), BF16),
        ],
        flops=2 * CHUNKS * tall * model * 2 * half,
    )


def up_body(*refs):
    pieces, (wg_ref, wu_ref) = refs[:6], refs[6:8]
    mid_ref, gate_ref, up_ref, hidden_ref = refs[-4:]
    rows = pieces[0].shape[0]

    @pl.when(pl.program_id(0) == 0)
    def _():
        def store(i, value):
            mid_ref[0, i * rows : (i + 1) * rows] = value

        load_pieces(pieces, store)

    gate = dot(mid_ref[0], wg_ref[...])
    up = dot(mid_ref[0], wu_ref[...])
    gate_ref[0] = gate.astype(gate_ref.dtype)
    up_ref[0] = up.astype(up_ref.dtype)
    hidden_ref[0] = (gate * jax.nn.sigmoid(gate) * up).astype(BF16)


def up_call(x, pieces, w_gate, w_up, prev):
    rows, model = pieces[0].shape
    hidden = w_gate.shape[1]
    extra, extra_specs, alias = chain(prev, 8, range(4))
    block = spec((1, 4 * rows, NCOL), x, 0, None)
    return call(
        up_body,
        *pieces,
        w_gate,
        w_up,
        *extra,
        grid=(hidden // NCOL,),
        in_specs=[whole((rows, model))] * 6 + [spec((model, NCOL), 0, None)] * 2 + extra_specs,
        out_specs=[spec((1, 4 * rows, model), x, 0, 0), block, block, block],
        out_shape=[struct((CHUNKS, 4 * rows, model), BF16)]
        + [struct((CHUNKS, 4 * rows, hidden), BF16)] * 3,
        alias=alias,
        flops=4 * 4 * rows * model * hidden,
    )


def down_body(hidden_ref, w_ref, *outs):
    value = dot(hidden_ref[0], w_ref[...])
    rows = outs[0].shape[0]
    for i, out in enumerate(outs):
        out[...] = value[i * rows : (i + 1) * rows].astype(out.dtype)


def down_call(x, hidden, w_down):
    _, tall, ff = hidden.shape
    model = w_down.shape[1]
    rows = tall // 4
    return call(
        down_body,
        hidden,
        w_down,
        grid=(model // NCOL,),
        in_specs=[spec((1, tall, ff), x, 0, 0), spec((ff, NCOL), 0, None)],
        out_specs=[spec((rows, NCOL), 0, None)] * 4,
        out_shape=[struct((rows, model), t) for t in (F32, BF16, BF16, BF16)],
        flops=2 * tall * ff * model,
    )


def dhid_body(*refs):
    pieces, (w_ref, gate_ref, up_ref) = refs[:6], refs[6:9]
    dm_ref, dg_ref, du_ref = refs[-3:]
    rows = pieces[0].shape[0]

    @pl.when(pl.program_id(0) == 0)
    def _():
        def store(i, value):
            dm_ref[0, i * rows : (i + 1) * rows] = value

        load_pieces(pieces, store)

    dh = dot(dm_ref[0], w_ref[...], COLS)
    gate = gate_ref[0].astype(F32)
    up = up_ref[0].astype(F32)
    sig = jax.nn.sigmoid(gate)
    scaled = dh * sig
    du_ref[0] = (scaled * gate).astype(BF16)
    dg_ref[0] = (scaled * up * (1.0 + gate * (1.0 - sig))).astype(BF16)


def dhid_call(x, pieces, w_down, gate, up, prev):
    rows, model = pieces[0].shape
    ff = w_down.shape[0]
    extra, extra_specs, alias = chain(prev, 9, range(3))
    block = spec((1, 4 * rows, NCOL), x, 0, None)
    return call(
        dhid_body,
        *pieces,
        w_down,
        gate,
        up,
        *extra,
        grid=(ff // NCOL,),
        in_specs=[whole((rows, model))] * 6
        + [spec((NCOL, model), None, 0), block, block]
        + extra_specs,
        out_specs=[spec((1, 4 * rows, model), x, 0, 0), block, block],
        out_shape=[struct((CHUNKS, 4 * rows, model), BF16)]
        + [struct((CHUNKS, 4 * rows, ff), BF16)] * 2,
        alias=alias,
        flops=2 * 4 * rows * model * ff,
    )


def dres_body(dg_ref, du_ref, wg_ref, wu_ref, *outs):
    value = dot(dg_ref[0], wg_ref[...], COLS) + dot(du_ref[0], wu_ref[...], COLS)
    rows = outs[0].shape[0]
    for i, out in enumerate(outs):
        out[...] = value[i * rows : (i + 1) * rows].astype(out.dtype)


def dres_call(x, dg, du, w_gate, w_up):
    _, tall, ff = dg.shape
    model = w_gate.shape[0]
    rows = tall // 4
    return call(
        dres_body,
        dg,
        du,
        w_gate,
        w_up,
        grid=(model // NCOL,),
        in_specs=[spec((1, tall, ff), x, 0, 0)] * 2 + [spec((NCOL, ff), None, 0)] * 2,
        out_specs=[spec((rows, NCOL), 0, None)] * 4,
        out_shape=[struct((rows, model), t) for t in (F32, BF16, BF16, BF16)],
        flops=4 * tall * ff * model,
    )


def scaled(value):
    rs = lax.rsqrt(jnp.mean(value * value, axis=1, keepdims=True) + norm_eps)
    return rs, value * rs


def post_attn_body(own, e1, m2, tok_ref, gain_ref, res_ref, mid_ref, part_ref):
    value = own[...] + e1[...].astype(F32) + m2[...].astype(F32)
    part_ref[...] = value
    _, hat = scaled(value)
    residual = tok_ref[...].astype(F32) + hat * gain_ref[...]
    res_ref[...] = residual
    mid_ref[...] = residual.astype(BF16)


def post_attn(x, terms, tokens, gain):
    rows, model = terms[0].shape
    return call(
        post_attn_body,
        *terms,
        tokens,
        gain,
        grid=(1,),
        in_specs=[whole((rows, model))] * 3 + [spec((rows, model), x, 0), whole((1, model))],
        out_specs=[whole((rows, model))] * 3,
        out_shape=[struct((rows, model), t) for t in (F32, BF16, F32)],
        flops=1e6,
    )


def post_mlp_body(own, e1, m2, res_ref, cot_ref, gain_ref, *refs):
    out_ref, dm_ref, part_ref = refs[-3:]
    value = own[...] + e1[...].astype(F32) + m2[...].astype(F32)
    rs, hat = scaled(value)
    gain = gain_ref[...]
    out_ref[...] = (res_ref[...] + hat * gain).astype(BF16)
    upstream = cot_ref[...].astype(F32)
    both = upstream * hat
    part_ref[...] = jnp.sum(both, axis=0, keepdims=True)
    mean = jnp.mean(both * gain, axis=1, keepdims=True)
    dm_ref[...] = (rs * (upstream * gain - hat * mean)).astype(BF16)


def post_mlp(x, terms, residual, cotangent, gain, prev):
    rows, model = terms[0].shape
    extra, extra_specs, alias = chain(prev, 6, (0,))
    return call(
        post_mlp_body,
        *terms,
        residual,
        cotangent,
        gain,
        *extra,
        grid=(1,),
        in_specs=[whole((rows, model))] * 4
        + [spec((rows, model), x, 0), whole((1, model))]
        + extra_specs,
        out_specs=[spec((rows, model), x, 0), whole((rows, model)), whole((1, model))],
        out_shape=[
            struct((CHUNKS * rows, model), BF16),
            struct((rows, model), BF16),
            struct((1, model), F32),
        ],
        alias=alias,
        flops=1e6,
    )


def post_bwd_body(own, e1, m2, cot_ref, attn_ref, gain_ref, dres_ref, da_ref, part_ref):
    value = own[...] + e1[...].astype(F32) + m2[...].astype(F32)
    value = value + cot_ref[...].astype(F32)
    dres_ref[...] = value
    rs, hat = scaled(attn_ref[...])
    gain = gain_ref[...]
    both = value * hat
    part_ref[...] = jnp.sum(both, axis=0, keepdims=True)
    mean = jnp.mean(both * gain, axis=1, keepdims=True)
    da_ref[...] = (rs * (value * gain - hat * mean)).astype(BF16)


def post_bwd(x, terms, cotangent, attn_part, gain):
    rows, model = terms[0].shape
    return call(
        post_bwd_body,
        *terms,
        cotangent,
        attn_part,
        gain,
        grid=(1,),
        in_specs=[whole((rows, model))] * 3
        + [spec((rows, model), x, 0), whole((rows, model)), whole((1, model))],
        out_specs=[whole((rows, model)), whole((rows, model)), whole((1, model))],
        out_shape=[
            struct((rows, model), F32),
            struct((rows, model), BF16),
            struct((1, model), F32),
        ],
        flops=1e6,
    )


def last_body(own, e1, m2, dres_ref, *refs):
    value = own[...] + e1[...].astype(F32) + m2[...].astype(F32)
    refs[-1][...] = dres_ref[...] + value


def last(x, terms, d_residual, prev):
    rows, model = terms[0].shape
    extra, extra_specs, alias = chain(prev, 4, (0,))
    return call(
        last_body,
        *terms,
        d_residual,
        *extra,
        grid=(1,),
        in_specs=[whole((rows, model))] * 4 + extra_specs,
        out_specs=[spec((rows, model), x, 0)],
        out_shape=[struct((CHUNKS * rows, model), F32)],
        alias=alias,
        flops=1e6,
    )


def on_device(
    n_dp,
    tokens,
    w_query,
    w_key,
    w_value,
    w_out,
    w_gate,
    w_up,
    w_down,
    query_gain,
    key_gain,
    attn_gain,
    mlp_gain,
    cotangent,
):
    return layer(
        n_dp,
        tokens,
        w_query,
        w_key,
        w_value,
        w_out,
        w_gate,
        w_up,
        w_down,
        query_gain,
        key_gain,
        attn_gain,
        mlp_gain,
        cotangent,
    )


def layer(
    n_dp,
    tokens,
    w_query,
    w_key,
    w_value,
    w_out,
    w_gate,
    w_up,
    w_down,
    query_gain,
    key_gain,
    attn_gain,
    mlp_gain,
    cotangent,
):
    fast = n_dp == BLOCKS
    all_rows, model = tokens.shape
    rows = all_rows // CHUNKS
    length = 4 * all_rows
    heads, gain_part = query_gain.shape
    head = gain_part * n_dp
    width = heads * head
    half = 3 * width // 2
    t = lax.axis_index("tensor")
    d = lax.axis_index("dp")

    third = jnp.where(t < 2, 2, 1)
    fourth = jnp.where(t < 2, 3, 0)
    sid = jnp.stack([t, t ^ 1, third, fourth]).astype(jnp.int32)
    slots = jnp.arange(4, dtype=jnp.int32)
    inv = jnp.sum(jnp.where(sid[None, :] == slots[:, None], slots[None, :], 0), axis=1)
    inv = inv.astype(jnp.int32)

    small = [query_gain.reshape(-1), key_gain.reshape(-1), attn_gain, mlp_gain]
    sizes = [s.shape[0] for s in small]
    extra = 16
    flat = jnp.concatenate(small)
    row = jnp.pad(flat[None, :], ((0, extra - 1), (0, half - flat.shape[0])))
    packed = jnp.concatenate([w_query, w_key, w_value], axis=1)
    pack_a = jnp.concatenate([packed[:, :half], row], axis=0)
    pack_b = packed[:, half:]
    if fast:
        xord = d.astype(jnp.int32) ^ jnp.array(ORDER, jnp.int32)
        a1 = jnp.stack([pack_a, flip(pack_a, BIT_X)])
        b1 = jnp.stack([pack_b, flip(pack_b, BIT_Y)])
        a2 = jnp.concatenate([a1, flip(a1, BIT_Y)])
        b2 = jnp.stack([b1, flip(b1, BIT_X)], axis=1).reshape(4, *pack_b.shape)
        a3 = flip(a2, BIT_CORE)
        b3 = flip(b2, BIT_CORE)
        weights = (a2, a3, b2, b3)
        rel = jnp.concatenate([a2[:, -extra], a3[:, -extra]])
        place = jnp.zeros((BLOCKS,), jnp.int32).at[xord].set(jnp.arange(BLOCKS, dtype=jnp.int32))
        gains = jnp.take(rel, place, axis=0)
    else:
        xord = jnp.arange(BLOCKS, dtype=jnp.int32)
        all_a = lax.all_gather(pack_a, "dp", axis=0)
        all_b = lax.all_gather(pack_b, "dp", axis=0)
        wide_a = all_a[:, :-extra].reshape(BLOCKS, -1, half)
        wide_b = all_b.reshape(BLOCKS, -1, half)
        weights = (wide_a[:4], wide_a[4:], wide_b[:4], wide_b[4:])
        gains = all_a[:, -extra]
    at = [sum(sizes[:i]) for i in range(5)]

    def head_gain(values):
        values = values.reshape(n_dp, heads, gain_part).transpose(1, 0, 2)
        return values.reshape(heads, 1, head).astype(F32)

    gain_q = head_gain(gains[:, at[0] : at[1]])
    gain_k = head_gain(gains[:, at[1] : at[2]])
    gain_attn = gains[:, at[2] : at[3]].reshape(1, model).astype(F32)
    gain_mlp = gains[:, at[3] : at[4]].reshape(1, model).astype(F32)

    full_out = lax.all_gather(w_out, "dp", axis=1, tiled=True)
    full_gate = lax.all_gather(w_gate, "dp", axis=0, tiled=True)
    full_up = lax.all_gather(w_up, "dp", axis=0, tiled=True)
    full_down = lax.all_gather(w_down, "dp", axis=1, tiled=True)

    cos, sin = rope_tables(length, head)
    turns = range(CHUNKS)

    token_pieces = [line_gather(tokens[x * rows : (x + 1) * rows]) for x in turns]
    prev = None
    for x in turns:
        prev = qkv_call(x, token_pieces[x], weights, sid, xord, prev, width)
    qk, v, xs, sums = prev
    sums = [sums, *everyone(sums)]
    qrot, krot, ctx, lse, rq, rk = attn_fwd(
        inv, qk, v, sums, gain_q, gain_k, cos, sin, model
    )
    after_attn = []
    for x in turns:
        terms = line_scatter(out_call(x, ctx, full_out))
        after_attn.append(post_attn(x, terms, tokens, gain_attn))

    prev = None
    outs = None
    mlp_parts = []
    d_mlp = []
    for x in turns:
        pieces = line_gather(after_attn[x][1])
        prev = up_call(x, pieces, full_gate, full_up, prev)
        terms = line_scatter(down_call(x, prev[3], full_down))
        outs, dm, part = post_mlp(
            x, terms, after_attn[x][0], cotangent, gain_mlp, outs and outs[:1]
        )
        outs = (outs,)
        d_mlp.append(dm)
        mlp_parts.append(part)
    mids, gates, ups, hiddens = prev
    layer_output = outs[0]

    prev = None
    d_res, d_attn, attn_parts = [], [], []
    for x in turns:
        pieces = line_gather(d_mlp[x])
        prev = dhid_call(x, pieces, full_down, gates, ups, prev)
        terms = line_scatter(dres_call(x, prev[1], prev[2], full_gate, full_up))
        dr, da, part = post_bwd(x, terms, cotangent, after_attn[x][2], gain_attn)
        d_res.append(dr)
        d_attn.append(da)
        attn_parts.append(part)
    dms, d_gates, d_ups = prev
    flat_rows = lambda a: a.reshape(length, a.shape[2])
    grad_down = dot(flat_rows(hiddens), flat_rows(dms), ROWS, BF16)
    grad_gate = dot(flat_rows(mids), flat_rows(d_gates), ROWS, BF16)
    grad_up = dot(flat_rows(mids), flat_rows(d_ups), ROWS, BF16)
    grad_down = lax.psum_scatter(grad_down, "dp", scatter_dimension=1, tiled=True)
    grad_gate = lax.psum_scatter(grad_gate, "dp", scatter_dimension=0, tiled=True)
    grad_up = lax.psum_scatter(grad_up, "dp", scatter_dimension=0, tiled=True)

    prev = None
    for x in turns:
        prev = dctx_call(x, line_gather(d_attn[x]), full_out, prev)
    dctx, das = prev
    grad_out = gout_call(ctx, das)
    grad_out = lax.psum_scatter(grad_out, "dp", scatter_dimension=1, tiled=True)
    lanes = 4 * rows
    gain_sums = jnp.concatenate([sum(attn_parts), sum(mlp_parts)]).reshape(-1, lanes)
    gq, gk, dv, head_gains, dots = attn_bwd(
        inv, qrot, krot, v, dctx, ctx, lse, qk, rq, rk, gain_q, gain_k, cos, sin, gain_sums
    )
    dots = [dots, *everyone(dots)]
    prev = None
    grad_tokens = None
    for x in turns:
        *parts, dqkv = dinput_call(
            x, dots, gq, gk, dv, qk, rq, rk, weights, sid, xord, prev, model
        )
        prev = (dqkv,)
        terms = line_scatter(parts)
        grad_tokens = last(x, terms, d_res[x], grad_tokens)
    grad_tokens = grad_tokens[0]

    gain_sums = sum(a[8 * CHUNKS :] for a in dots).reshape(2, n_dp, -1)

    def spread(values):
        values = values.reshape(heads, n_dp, gain_part).transpose(1, 0, 2)
        return values.reshape(n_dp, heads * gain_part)

    gain_rows = jnp.concatenate(
        [spread(head_gains[:, 0]), spread(head_gains[:, 1]), gain_sums[0], gain_sums[1]], axis=1
    )
    gain_rows = jnp.pad(gain_rows, ((0, 0), (0, half - gain_rows.shape[1])))
    if fast:
        packed_gains = jnp.pad(gain_rows[:, None, :], ((0, 0), (0, extra - 1), (0, 0)))
        spot_a = {p: j for j, p in enumerate((0, 4, 2, 6, 1, 5, 3, 7))}
        spot_b = {p: j for j, p in enumerate((0, 2, 4, 6, 1, 3, 5, 7))}
        posa = jnp.array([spot_a[p] for p in ORDER], jnp.int32)
        posb = jnp.array([spot_b[p] for p in ORDER], jnp.int32)
        g_a, g_b = wgrad_call(xs, dqkv, packed_gains.astype(BF16), xord, posa, posb)
        for bits in ((BIT_CORE, BIT_CORE), (BIT_X, BIT_Y), (BIT_Y, BIT_X)):
            n = g_a.shape[0] // 2
            g_a = g_a[:n] + flip(g_a[n:], bits[0])
            g_b = g_b[:n] + flip(g_b[n:], bits[1])
        g_a, g_b = g_a[0], g_b[0]
        gain_row = g_a[-extra].astype(F32)
        g_a = g_a[:-extra]
    else:
        spots = jnp.arange(BLOCKS, dtype=jnp.int32)
        packed_gains = jnp.zeros((BLOCKS, extra, half), BF16)
        g_a, g_b = wgrad_call(xs, dqkv, packed_gains, xord, spots, spots)
        g_a = g_a[:, :-extra].reshape(model, half)
        g_b = g_b.reshape(model, half)
        g_a = lax.psum_scatter(g_a, "dp", scatter_dimension=0, tiled=True)
        g_b = lax.psum_scatter(g_b, "dp", scatter_dimension=0, tiled=True)
        gain_row = lax.psum_scatter(gain_rows, "dp", scatter_dimension=0, tiled=True)[0]
    grad_qkv = jnp.concatenate([g_a, g_b], axis=1).astype(F32)
    return (
        layer_output,
        grad_tokens,
        grad_qkv[:, :width],
        grad_qkv[:, width : 2 * width],
        grad_qkv[:, 2 * width :],
        grad_out.astype(F32),
        grad_gate.astype(F32),
        grad_up.astype(F32),
        grad_down.astype(F32),
        gain_row[at[0] : at[1]].reshape(heads, gain_part),
        gain_row[at[1] : at[2]].reshape(heads, gain_part),
        gain_row[at[2] : at[3]],
        gain_row[at[3] : at[4]],
    )


def solution(mesh):
    in_specs = (
        P(("dp", "tensor"), None),
        P("dp", "tensor"),
        P("dp", "tensor"),
        P("dp", "tensor"),
        P("tensor", "dp"),
        P("dp", "tensor"),
        P("dp", "tensor"),
        P("tensor", "dp"),
        P("tensor", "dp"),
        P("tensor", "dp"),
        P("dp"),
        P("dp"),
        P(("dp", "tensor"), None),
    )
    out_specs = (
        P(("dp", "tensor"), None),
        P(("dp", "tensor"), None),
        P("dp", "tensor"),
        P("dp", "tensor"),
        P("dp", "tensor"),
        P("tensor", "dp"),
        P("dp", "tensor"),
        P("dp", "tensor"),
        P("tensor", "dp"),
        P("tensor", "dp"),
        P("tensor", "dp"),
        P("dp"),
        P("dp"),
    )
    assert mesh.shape["tensor"] == 4
    return jax.shard_map(
        functools.partial(on_device, mesh.shape["dp"]),
        mesh=mesh,
        in_specs=in_specs,
        out_specs=out_specs,
        check_vma=False,
    )
```

```python
import functools
import math

import jax
import jax.numpy as jnp
from jax import lax
from jax.experimental import pallas as pl
from jax.experimental.pallas import tpu as pltpu
from jax.sharding import PartitionSpec as P


rope_theta = 500000.0
norm_eps = 1e-06

TP, DP = "tensor", "dp"
F32 = jnp.float32
BF16 = jnp.bfloat16

PAIRS = [(0, 1), (1, 0), (2, 3), (3, 2)]
MIDDLE = [(1, 2), (2, 1)]
OUTWARD = [(2, 3), (1, 0)]
INWARD = [(3, 2), (0, 1)]

ORDER = (0, 2, 4, 6, 1, 3, 5, 7)
BLOCKS = 8
BIT_CORE, BIT_X, BIT_Y = 1, 2, 4
CHUNKS = 2
NCOL = 512
STRIPS = 1

COLS = ((1,), (1,))
ROWS = ((0,), (0,))


def rope_tables(length, head_size):
    half_size = head_size // 2
    freqs = rope_theta ** (-(jnp.arange(half_size, dtype=F32) * 2.0) / head_size)
    angles = jnp.arange(length, dtype=F32)[:, None] * freqs[None, :]
    cosine, sine = jnp.cos(angles), jnp.sin(angles)
    return (
        jnp.concatenate([cosine, cosine], axis=1),
        jnp.concatenate([-sine, sine], axis=1),
    )


def shift(value, pairs):
    return lax.ppermute(value, TP, pairs)


def line_gather(own):
    e1 = shift(own, PAIRS)
    m_own = shift(own, MIDDLE)
    m_e1 = shift(e1, MIDDLE)
    f_own = shift(m_own, OUTWARD)
    f_e1 = shift(m_e1, OUTWARD)
    return own, e1, m_own, f_own, m_e1, f_e1


def line_scatter(parts):
    own, p1, p2, p3 = parts
    b3 = shift(p3, INWARD)
    b2 = shift(p2, INWARD)
    s3 = p3 + b3
    m3 = shift(s3, MIDDLE)
    s2 = p2 + b2
    m2 = shift(s2, MIDDLE)
    s1 = p1 + m3
    e1 = shift(s1, PAIRS)
    return own, e1, m2


def everyone(value):
    return [shift(value, [(i, (i + k) % 4) for i in range(4)]) for k in (1, 2, 3)]


def flip(value, bit):
    return lax.ppermute(value, DP, [(i, i ^ bit) for i in range(8)])


def dot(a, b, dims=((1,), (0,)), out=F32):
    return lax.dot_general(a, b, (dims, ((), ())), preferred_element_type=F32).astype(out)


def call(body, *args, grid, in_specs, out_specs, out_shape, flops, prefetch=0, **kw):
    scratch = kw.pop("scratch", [])
    size = sum(math.prod(a.shape) * a.dtype.itemsize for a in args)
    size += sum(math.prod(s.shape) * s.dtype.itemsize for s in out_shape)
    return pl.pallas_call(
        body,
        out_shape=out_shape,
        grid_spec=pltpu.PrefetchScalarGridSpec(
            num_scalar_prefetch=prefetch,
            grid=grid,
            in_specs=in_specs,
            out_specs=out_specs,
            scratch_shapes=scratch,
        ),
        input_output_aliases=kw.pop("alias", {}),
        compiler_params=pltpu.CompilerParams(
            dimension_semantics=("arbitrary",) * len(grid)
        ),
        cost_estimate=pl.CostEstimate(
            flops=int(flops), transcendentals=0, bytes_accessed=int(size)
        ),
    )(*args)


ANY = pl.BlockSpec(memory_space=pl.ANY)


def whole(shape):
    return pl.BlockSpec(shape, lambda *_: (0,) * len(shape))


def spec(shape, *at):
    return pl.BlockSpec(shape, lambda j, *_: tuple(j if a is None else a for a in at))


def struct(shape, dtype):
    return jax.ShapeDtypeStruct(shape, dtype)


def chain(prev, at, shapes):
    if prev is None:
        return [], [], {}
    return list(prev), [ANY] * len(prev), {at + i: o for i, o in enumerate(shapes)}


def load_pieces(refs, store, sid_ref=None):
    if len(refs) == 1:
        rows = refs[0].shape[0] // 4
        for i in range(4):
            at = pl.multiple_of(sid_ref[i] * rows, rows)
            store(i, refs[0][pl.ds(at, rows)])
        return
    own, e1, m_own, f_own, m_e1, f_e1 = refs
    store(0, own[...])
    store(1, e1[...])
    store(2, m_own[...] + f_own[...])
    store(3, m_e1[...] + f_e1[...])


def qkv_body(x_at, has_prev, sid_ref, xord_ref, *refs):
    pieces = refs[:6]
    alo, ahi, blo, bhi = refs[6:10]
    refs = refs[10:]
    if has_prev:
        prev_sums = refs[0]
        refs = refs[4:]
    qk_ref, v_ref, x_ref, sums_ref, xs, sq = refs
    step = pl.program_id(0)
    rows, model = pieces[0].shape
    kb = model // BLOCKS
    cols = alo.shape[2]

    @pl.when(step == 0)
    def _():
        def store(i, value):
            x_ref[0, i * rows : (i + 1) * rows] = value

        load_pieces(pieces, store)
        for j in range(BLOCKS):
            at = pl.multiple_of(xord_ref[j] * kb, kb)
            xs[:, j * kb : (j + 1) * kb] = x_ref[0, :, pl.ds(at, kb)]
        sq[...] = jnp.zeros_like(sq)

    def work(lo_ref, hi_ref):
        low = lo_ref[...].reshape(4 * kb, cols)
        high = hi_ref[...].reshape(4 * kb, cols)
        value = dot(xs[:, : 4 * kb], low) + dot(xs[:, 4 * kb :], high)

        @pl.when(step < 4)
        def _():
            qk_ref[...] = value.reshape(qk_ref.shape)
            lane = lax.broadcasted_iota(jnp.int32, sq.shape, 1)
            row = jnp.sum(value * value, axis=1, keepdims=True)
            sq[...] += jnp.where(lane == step // 2, row, 0.0)

        @pl.when(step >= 4)
        def _():
            v_ref[...] = value.astype(BF16).reshape(v_ref.shape)

    @pl.when(step < 3)
    def _():
        work(alo, ahi)

    @pl.when(step >= 3)
    def _():
        work(blo, bhi)

    @pl.when(step == 5)
    def _():
        if has_prev:
            sums_ref[...] = prev_sums[...]
        else:
            sums_ref[...] = jnp.zeros_like(sums_ref)
        for i in range(4):
            flipped = sq[i * rows : (i + 1) * rows, :].T
            at = pl.multiple_of(sid_ref[i] * rows, rows)
            sums_ref[8 * x_at : 8 * x_at + 8, pl.ds(at, rows)] = flipped[:8]


def qkv_call(x, pieces, weights, sid, xord, prev, width):
    rows, model = pieces[0].shape
    kb = model // BLOCKS
    cols = width // 2
    shapes = (
        struct((4, CHUNKS * rows, 2 * width), F32),
        struct((4, CHUNKS * rows, width), BF16),
        struct((CHUNKS, 4 * rows, model), BF16),
        struct((8 * CHUNKS, 4 * rows), F32),
    )
    extra, extra_specs, alias = [], [], {}
    if prev is not None:
        extra = [prev[3], *prev[:3]]
        extra_specs = [whole(shapes[3].shape), ANY, ANY, ANY]
        alias = {13 + i: i for i in range(3)}
    weight = lambda at: pl.BlockSpec((4, kb, cols), lambda j, *_: (0, 0, at(j)))
    return call(
        functools.partial(qkv_body, x, prev is not None),
        sid,
        xord,
        *pieces,
        *weights,
        *extra,
        grid=(6,),
        prefetch=2,
        in_specs=[whole((rows, model))] * 6
        + [weight(lambda j: jnp.minimum(j, 2))] * 2
        + [weight(lambda j: jnp.maximum(j - 3, 0))] * 2
        + extra_specs,
        out_specs=[
            pl.BlockSpec((4, rows, cols), lambda j, *_: (0, x, jnp.minimum(j, 3))),
            pl.BlockSpec((4, rows, cols), lambda j, *_: (0, x, jnp.maximum(j - 4, 0))),
            spec((1, 4 * rows, model), x, 0, 0),
            whole(shapes[3].shape),
        ],
        out_shape=shapes,
        alias=alias,
        scratch=[pltpu.VMEM((4 * rows, model), BF16), pltpu.VMEM((4 * rows, 128), F32)],
        flops=2 * 4 * rows * model * 3 * width,
    )


def out_body(ctx_ref, w_ref, p0, p1, p2, p3):
    rows = ctx_ref.shape[1]
    value = dot(ctx_ref[...].reshape(4 * rows, -1), w_ref[...])
    for i, out in enumerate((p0, p1, p2, p3)):
        out[...] = value[i * rows : (i + 1) * rows].astype(out.dtype)


def out_call(x, ctx, w_out):
    _, all_rows, width = ctx.shape
    rows = all_rows // CHUNKS
    model = w_out.shape[1]
    return call(
        out_body,
        ctx,
        w_out,
        grid=(model // NCOL,),
        in_specs=[spec((4, rows, width), 0, x, 0), spec((width, NCOL), 0, None)],
        out_specs=[spec((rows, NCOL), 0, None)] * 4,
        out_shape=[struct((rows, model), t) for t in (F32, BF16, BF16, BF16)],
        flops=2 * 4 * rows * width * model,
    )


def dctx_body(*refs):
    pieces, w_ref, (ctx_ref, da_ref) = refs[:6], refs[6], refs[-2:]
    rows = pieces[0].shape[0]

    def store(i, value):
        da_ref[0, i * rows : (i + 1) * rows] = value

    load_pieces(pieces, store)
    ctx_ref[...] = dot(da_ref[0], w_ref[...], COLS, BF16).reshape(ctx_ref.shape)


def dctx_call(x, pieces, w_out, prev):
    rows, model = pieces[0].shape
    width = w_out.shape[0]
    extra, extra_specs, alias = chain(prev, 7, (0, 1))
    return call(
        dctx_body,
        *pieces,
        w_out,
        *extra,
        grid=(1,),
        in_specs=[whole((rows, model))] * 6 + [whole((width, model))] + extra_specs,
        out_specs=[spec((4, rows, width), 0, x, 0), spec((1, 4 * rows, model), x, 0, 0)],
        out_shape=[
            struct((4, CHUNKS * rows, width), BF16),
            struct((CHUNKS, 4 * rows, model), BF16),
        ],
        alias=alias,
        flops=2 * 4 * rows * width * model,
    )


def column(row):
    return jnp.broadcast_to(row, (128, row.shape[1])).T


def attn_fwd_body(
    scale,
    inv_model,
    inv_ref,
    q_ref,
    k_ref,
    v_ref,
    s0,
    s1,
    s2,
    s3,
    gq_ref,
    gk_ref,
    cos_ref,
    sin_ref,
    qrot_ref,
    krot_ref,
    ctx_ref,
    lse_ref,
    rq_ref,
    rk_ref,
):
    rows, head = q_ref.shape[1:]
    part = rows // CHUNKS
    gq, gk = gq_ref[0], gk_ref[0]

    @pl.when(pl.program_id(0) == 0)
    def _():
        rs = lax.rsqrt((s0[...] + s1[...] + s2[...] + s3[...]) * inv_model + norm_eps)
        for b in range(4):
            r = inv_ref[b]
            for x in range(CHUNKS):
                for out, at in ((rq_ref, 8 * x), (rk_ref, 8 * x + 1)):
                    out[r, x * part : (x + 1) * part] = column(
                        rs[at : at + 1, b * part : (b + 1) * part]
                    )

    for b in range(4):
        r = inv_ref[b]
        cos = cos_ref[b * rows : (b + 1) * rows]
        sin = sin_ref[b * rows : (b + 1) * rows]
        qn = q_ref[r] * rq_ref[r] * gq
        kn = k_ref[r] * rk_ref[r] * gk
        qrot_ref[r] = (qn * cos + pltpu.roll(qn, head // 2, 1) * sin).astype(BF16)
        krot_ref[r] = (kn * cos + pltpu.roll(kn, head // 2, 1) * sin).astype(BF16)
    causal = lax.broadcasted_iota(jnp.int32, (rows, rows), 0) >= lax.broadcasted_iota(
        jnp.int32, (rows, rows), 1
    )
    for b in range(4):
        r = inv_ref[b]
        q = qrot_ref[r]
        parts = []
        for c in range(b + 1):
            s = dot(q, krot_ref[inv_ref[c]], COLS) * scale
            if c == b:
                s = jnp.where(causal, s, -1e30)
            parts.append(s)
        top = jnp.max(parts[0], axis=1, keepdims=True)
        for s in parts[1:]:
            top = jnp.maximum(top, jnp.max(s, axis=1, keepdims=True))
        exps = [jnp.exp(s - top) for s in parts]
        total = jnp.sum(exps[0], axis=1, keepdims=True)
        for e in exps[1:]:
            total = total + jnp.sum(e, axis=1, keepdims=True)
        inverse = 1.0 / total
        ctx = None
        for c in range(b + 1):
            piece = dot((exps[c] * inverse).astype(BF16), v_ref[inv_ref[c]])
            ctx = piece if ctx is None else ctx + piece
        ctx_ref[r] = ctx.astype(BF16)
        lse_ref[0, r] = top + jnp.log(total)


def attn_fwd(inv, qk, v, sums, gq, gk, cos, sin, model):
    _, rows, width2 = qk.shape
    width = width2 // 2
    heads, _, head = gq.shape
    per_head = spec((4, rows, head), 0, 0, None)
    return call(
        functools.partial(attn_fwd_body, 1.0 / math.sqrt(head), 1.0 / model),
        inv,
        qk,
        qk,
        v,
        *sums,
        gq,
        gk,
        cos,
        sin,
        grid=(heads,),
        prefetch=1,
        in_specs=[
            per_head,
            pl.BlockSpec((4, rows, head), lambda h, iv: (0, 0, heads + h)),
            per_head,
        ]
        + [whole(sums[0].shape)] * 4
        + [spec((1, 1, head), None, 0, 0)] * 2
        + [whole(cos.shape)] * 2,
        out_specs=[per_head] * 3
        + [spec((1, 4, rows, 1), None, 0, 0, 0)]
        + [whole((4, rows, 128))] * 2,
        out_shape=[struct((4, rows, width), BF16)] * 3
        + [struct((heads, 4, rows, 1), F32)]
        + [struct((4, rows, 128), F32)] * 2,
        flops=4e9,
    )


def attn_bwd_body(
    scale,
    inv_ref,
    qrot_ref,
    krot_ref,
    v_ref,
    dctx_ref,
    ctx_ref,
    lse_ref,
    q_ref,
    k_ref,
    rq_ref,
    rk_ref,
    gq_ref,
    gk_ref,
    cos_ref,
    sin_ref,
    extra_ref,
    dq_ref,
    dk_ref,
    dv_ref,
    gain_ref,
    dots_ref,
    dk_acc,
    dv_acc,
    dots,
):
    rows, head = q_ref.shape[1:]
    part = rows // CHUNKS
    causal = lax.broadcasted_iota(jnp.int32, (rows, rows), 0) >= lax.broadcasted_iota(
        jnp.int32, (rows, rows), 1
    )
    lane = lax.broadcasted_iota(jnp.int32, (rows, 128), 1)
    gq, gk = gq_ref[0], gk_ref[0]
    first = pl.program_id(0) == 0

    def finish(raw, b, r, raw_ref, rs_ref, gain, out_ref):
        cos = cos_ref[b * rows : (b + 1) * rows]
        sin = sin_ref[b * rows : (b + 1) * rows]
        norm = raw * cos - pltpu.roll(raw, head // 2, 1) * sin
        hat = raw_ref[r] * rs_ref[r]
        both = norm * hat
        out_ref[r] = norm * gain
        return (
            jnp.sum(both, axis=0, keepdims=True),
            jnp.sum(both * gain, axis=1, keepdims=True),
        )

    q_gain = jnp.zeros((1, head), F32)
    k_gain = jnp.zeros((1, head), F32)
    q_dots = []
    for b in range(4):
        r = inv_ref[b]
        q = qrot_ref[r]
        dctx = dctx_ref[r]
        lse = lse_ref[0, r]
        delta = jnp.sum(dctx.astype(F32) * ctx_ref[r].astype(F32), axis=1, keepdims=True)
        dq = None
        for c in range(b + 1):
            rc = inv_ref[c]
            k = krot_ref[rc]
            s = dot(q, k, COLS) * scale
            if c == b:
                s = jnp.where(causal, s, -1e30)
            p = jnp.exp(s - lse)
            dp = dot(dctx, v_ref[rc], COLS)
            ds = (p * (dp - delta) * scale).astype(BF16)
            dv_part = dot(p.astype(BF16), dctx, ROWS)
            dk_part = dot(ds, q, ROWS)
            dq_part = dot(ds, k)
            dq = dq_part if dq is None else dq + dq_part
            if c == b:
                dv_acc[c] = dv_part
                dk_acc[c] = dk_part
            else:
                dv_acc[c] += dv_part
                dk_acc[c] += dk_part
        gain_part, row_dot = finish(dq, b, r, q_ref, rq_ref, gq, dq_ref)
        q_gain = q_gain + gain_part
        q_dots.append(row_dot)
    for b in range(4):
        r = inv_ref[b]
        gain_part, row_dot = finish(dk_acc[b], b, r, k_ref, rk_ref, gk, dk_ref)
        k_gain = k_gain + gain_part
        dv_ref[r] = dv_acc[b].astype(BF16)
        old = jnp.where(first, 0.0, dots[b])
        dots[b] = old + jnp.where(lane == 0, q_dots[b], jnp.where(lane == 1, row_dot, 0.0))
    row = lax.broadcasted_iota(jnp.int32, (8, head), 0)
    gain_ref[0] = jnp.where(row == 0, q_gain, jnp.where(row == 1, k_gain, 0.0))

    @pl.when(pl.program_id(0) == pl.num_programs(0) - 1)
    def _():
        for b in range(4):
            for x in range(CHUNKS):
                flipped = dots[b, x * part : (x + 1) * part].T
                dots_ref[8 * x : 8 * x + 8, b * part : (b + 1) * part] = flipped[:8]
        dots_ref[8 * CHUNKS :] = extra_ref[...]


def attn_bwd(inv, qrot, krot, v, dctx, ctx, lse, qk, rq, rk, gq, gk, cos, sin, extra):
    _, rows, width = qrot.shape
    heads, _, head = gq.shape
    per_head = spec((4, rows, head), 0, 0, None)
    dots_shape = (8 * CHUNKS + extra.shape[0], extra.shape[1])
    return call(
        functools.partial(attn_bwd_body, 1.0 / math.sqrt(head)),
        inv,
        qrot,
        krot,
        v,
        dctx,
        ctx,
        lse,
        qk,
        qk,
        rq,
        rk,
        gq,
        gk,
        cos,
        sin,
        extra,
        grid=(heads,),
        prefetch=1,
        in_specs=[per_head] * 5
        + [
            spec((1, 4, rows, 1), None, 0, 0, 0),
            per_head,
            pl.BlockSpec((4, rows, head), lambda h, iv: (0, 0, heads + h)),
        ]
        + [whole((4, rows, 128))] * 2
        + [spec((1, 1, head), None, 0, 0)] * 2
        + [whole(cos.shape)] * 2
        + [whole(extra.shape)],
        out_specs=[per_head] * 3
        + [spec((1, 8, head), None, 0, 0)]
        + [whole(dots_shape)],
        out_shape=[struct((4, rows, width), F32)] * 2
        + [
            struct((4, rows, width), BF16),
            struct((heads, 8, head), F32),
            struct(dots_shape, F32),
        ],
        scratch=[pltpu.VMEM((4, rows, head), F32)] * 2 + [pltpu.VMEM((4, rows, 128), F32)],
        flops=12e9,
    )


def dqkv_rows(inv_model, sid_ref, refs, out_ref):
    d0, d1, d2, d3, gq_ref, gk_ref, dv_ref, qk_ref, rq_ref, rk_ref = refs
    rows, width = gq_ref.shape[1] // CHUNKS, gq_ref.shape[2]
    total = (d0[...] + d1[...] + d2[...] + d3[...]) * inv_model
    for x in range(CHUNKS):
        span = slice(x * rows, (x + 1) * rows)
        for i in range(4):
            to = slice(i * rows, (i + 1) * rows)
            for g_ref, r_ref, row, at in (
                (gq_ref, rq_ref, 8 * x, 0),
                (gk_ref, rk_ref, 8 * x + 1, width),
            ):
                rs = r_ref[i, span]
                sums = jnp.zeros((1, rows), F32)
                for b in range(4):
                    here = total[row : row + 1, b * rows : (b + 1) * rows]
                    sums = jnp.where(sid_ref[i] == b, here, sums)
                mean = column(sums)
                for h in range(width // 128):
                    lo = at + h * 128
                    hat = qk_ref[i, span, lo : lo + 128] * rs
                    value = rs * (g_ref[i, span, h * 128 : (h + 1) * 128] - hat * mean)
                    out_ref[x, to, lo : lo + 128] = value.astype(BF16)
            out_ref[x, to, 2 * width :] = dv_ref[i, span]


def dinput_body(x, inv_model, sid_ref, xord_ref, *refs):
    step = pl.program_id(0)
    if x == 0:
        outs, d_ref = refs[-5:-1], refs[-1]
        weights = refs[10:14]

        @pl.when(step == 0)
        def _():
            dqkv_rows(inv_model, sid_ref, refs[:10], d_ref)
    else:
        outs, d_ref = refs[-4:], refs[0]
        weights = refs[1:5]
    alo, ahi, blo, bhi = weights
    rows = outs[0].shape[0]
    kb = alo.shape[1]
    half = alo.shape[2]

    def work(a_ref, b_ref):
        for q in range(2):
            value = dot(d_ref[0, :, :half], a_ref[q], COLS) + dot(
                d_ref[0, :, half:], b_ref[q], COLS
            )
            at = pl.multiple_of(xord_ref[2 * step + q] * kb, kb)
            for i, out in enumerate(outs):
                out[:, pl.ds(at, kb)] = value[i * rows : (i + 1) * rows].astype(out.dtype)

    @pl.when(step < 2)
    def _():
        work(alo, blo)

    @pl.when(step >= 2)
    def _():
        work(ahi, bhi)


def dinput_call(x, sources, weights, sid, xord, model):
    tall = sources[0].shape[1] if x else 4 * sources[4].shape[1] // CHUNKS
    cols = 2 * weights[0].shape[2]
    rows = tall // 4
    kb = model // BLOCKS
    low = pl.BlockSpec((2, kb, cols // 2), lambda j, *_: (jnp.minimum(j, 1), 0, 0))
    high = pl.BlockSpec((2, kb, cols // 2), lambda j, *_: (jnp.maximum(j - 2, 0), 0, 0))
    out_specs = [whole((rows, model))] * 4
    out_shape = [struct((rows, model), t) for t in (F32, BF16, BF16, BF16)]
    if x == 0:
        in_specs = [whole(a.shape) for a in sources]
        out_specs = [*out_specs, whole((CHUNKS, tall, cols))]
        out_shape = [*out_shape, struct((CHUNKS, tall, cols), BF16)]
    else:
        in_specs = [spec((1, tall, cols), x, 0, 0)]
    return call(
        functools.partial(dinput_body, x, 1.0 / model),
        sid,
        xord,
        *sources,
        *weights,
        grid=(4,),
        prefetch=2,
        in_specs=in_specs + [low, high, low, high],
        out_specs=out_specs,
        out_shape=out_shape,
        flops=2 * tall * model * cols,
    )


def wgrad_body(xord_ref, posa_ref, x_ref, d_ref, ctx_ref, da_ref, g_ref, a_ref, b_ref, ctx_t):
    kb = x_ref.shape[2]
    half = d_ref.shape[2] // 2
    rows = ctx_ref.shape[1] // CHUNKS

    @pl.when(pl.program_id(0) == 0)
    def _():
        for x in range(CHUNKS):
            for i in range(4):
                at = (4 * x + i) * rows
                ctx_t[:, at : at + rows] = ctx_ref[i, x * rows : (x + 1) * rows].T

    flipped = [x_ref[x].T for x in range(CHUNKS)]
    for out, lo in ((a_ref, 0), (b_ref, half)):
        total = None
        for x in range(CHUNKS):
            part = dot(flipped[x], d_ref[x, :, lo : lo + half])
            total = part if total is None else total + part
        out[0, :kb, :half] = total.astype(BF16)
    value = dot(ctx_t[...], da_ref[...].reshape(ctx_t.shape[1], kb), out=BF16)
    tall = b_ref.shape[1]
    for i, out in enumerate((a_ref, b_ref)):
        out[0, :kb, half:] = value[i * tall : (i + 1) * tall]
    a_ref[0, kb:] = g_ref[0]


def wgrad_call(part, xs, dqkv, ctx, das, gains, xord, posa):
    _, tall, model = xs.shape
    kb = model // BLOCKS
    half = dqkv.shape[2] // 2
    extra, cols = gains.shape[1:]
    n = BLOCKS // 2
    return call(
        wgrad_body,
        xord,
        posa,
        xs,
        dqkv,
        ctx,
        das,
        gains,
        grid=(n,),
        prefetch=2,
        in_specs=[
            pl.BlockSpec((CHUNKS, tall, kb), lambda j, xo, pa: (0, 0, xo[n * part + j])),
            whole(dqkv.shape),
            whole(ctx.shape),
            pl.BlockSpec((CHUNKS, tall, kb), lambda j, xo, pa: (0, 0, xo[n * part + j])),
            pl.BlockSpec((1, extra, cols), lambda j, xo, pa: (xo[n * part + j], 0, 0)),
        ],
        out_specs=[
            pl.BlockSpec((1, kb + extra, cols), lambda j, xo, pa: (pa[j], 0, 0)),
            spec((1, kb, cols), None, 0, 0),
        ],
        out_shape=[struct((n, kb + extra, cols), BF16), struct((n, kb, cols), BF16)],
        scratch=[pltpu.VMEM((ctx.shape[2], CHUNKS * tall), BF16)],
        flops=CHUNKS * tall * model * (2 * half + ctx.shape[2]),
    )


def up_body(n, sid_ref, *refs):
    pieces, (wg_ref, wu_ref) = refs[:n], refs[n : n + 2]
    mid_ref, gate_ref, up_ref, hidden_ref = refs[-4:]
    rows = mid_ref.shape[1] // 4

    @pl.when(pl.program_id(0) == 0)
    def _():
        def store(i, value):
            mid_ref[0, i * rows : (i + 1) * rows] = value

        load_pieces(pieces, store, sid_ref)

    gate = dot(mid_ref[0], wg_ref[...])
    up = dot(mid_ref[0], wu_ref[...])
    gate_ref[0] = gate.astype(gate_ref.dtype)
    up_ref[0] = up.astype(up_ref.dtype)
    hidden_ref[0] = (gate * jax.nn.sigmoid(gate) * up).astype(BF16)


def up_call(x, pieces, w_gate, w_up, sid, prev):
    n = len(pieces)
    rows, model = pieces[0].shape
    rows = rows if n > 1 else rows // 4
    hidden = w_gate.shape[1]
    extra, extra_specs, alias = chain(prev, n + 3, range(4))
    block = spec((1, 4 * rows, NCOL), x, 0, None)
    return call(
        functools.partial(up_body, n),
        sid,
        *pieces,
        w_gate,
        w_up,
        *extra,
        grid=(hidden // NCOL,),
        prefetch=1,
        in_specs=[whole(pieces[0].shape)] * n + [spec((model, NCOL), 0, None)] * 2 + extra_specs,
        out_specs=[spec((1, 4 * rows, model), x, 0, 0), block, block, block],
        out_shape=[struct((CHUNKS, 4 * rows, model), BF16)]
        + [struct((CHUNKS, 4 * rows, hidden), BF16)] * 3,
        alias=alias,
        flops=4 * 4 * rows * model * hidden,
    )


def store_pieces(value, outs):
    rows = outs[0].shape[0]
    for i, out in enumerate(outs):
        out[...] = value[i * rows : (i + 1) * rows].astype(out.dtype)


def down_body(hidden_ref, w_ref, *outs):
    store_pieces(dot(hidden_ref[0], w_ref[...]), outs)


def down_call(x, hidden, w_down):
    _, tall, ff = hidden.shape
    model = w_down.shape[1]
    rows = tall // 4
    return call(
        down_body,
        hidden,
        w_down,
        grid=(model // NCOL,),
        in_specs=[spec((1, tall, ff), x, 0, 0), spec((ff, NCOL), 0, None)],
        out_specs=[spec((rows, NCOL), 0, None)] * 4,
        out_shape=[struct((rows, model), t) for t in (F32, BF16, BF16, BF16)],
        flops=2 * tall * ff * model,
    )


def dhid_body(n, sid_ref, *refs):
    pieces, (w_ref, gate_ref, up_ref) = refs[:n], refs[n : n + 3]
    dm_ref, dg_ref, du_ref = refs[-3:]
    rows = dm_ref.shape[1] // 4

    @pl.when(pl.program_id(0) == 0)
    def _():
        def store(i, value):
            dm_ref[0, i * rows : (i + 1) * rows] = value

        load_pieces(pieces, store, sid_ref)

    dh = dot(dm_ref[0], w_ref[...], COLS)
    gate = gate_ref[0].astype(F32)
    up = up_ref[0].astype(F32)
    sig = jax.nn.sigmoid(gate)
    scaled = dh * sig
    du_ref[0] = (scaled * gate).astype(BF16)
    dg_ref[0] = (scaled * up * (1.0 + gate * (1.0 - sig))).astype(BF16)


def dhid_call(x, pieces, w_down, gate, up, sid, prev):
    n = len(pieces)
    rows, model = pieces[0].shape
    rows = rows if n > 1 else rows // 4
    ff = w_down.shape[0]
    extra, extra_specs, alias = chain(prev, n + 4, range(3))
    block = spec((1, 4 * rows, NCOL), x, 0, None)
    return call(
        functools.partial(dhid_body, n),
        sid,
        *pieces,
        w_down,
        gate,
        up,
        *extra,
        grid=(ff // NCOL,),
        prefetch=1,
        in_specs=[whole(pieces[0].shape)] * n
        + [spec((NCOL, model), None, 0), block, block]
        + extra_specs,
        out_specs=[spec((1, 4 * rows, model), x, 0, 0), block, block],
        out_shape=[struct((CHUNKS, 4 * rows, model), BF16)]
        + [struct((CHUNKS, 4 * rows, ff), BF16)] * 2,
        alias=alias,
        flops=2 * 4 * rows * model * ff,
    )


def ggate_body(xord_ref, posa_ref, x0_ref, x1_ref, d_ref, ak, as_, bk, bs, flipped):
    step = pl.program_id(0)
    tall, kb = x0_ref.shape[1:]
    for x in range(CHUNKS):
        for q, ref in enumerate((x0_ref, x1_ref)):
            flipped[q * kb : (q + 1) * kb, x * tall : (x + 1) * tall] = ref[x].T
    cols = ak.shape[2]
    for lo, keep, send in ((0, ak, as_), (cols, bk, bs)):
        right = d_ref[:, :, lo : lo + cols].reshape(CHUNKS * tall, cols)
        value = dot(flipped[...], right, out=BF16)
        for q in range(2):
            at = lax.rem(2 * step + q, BLOCKS // 2)
            if lo == 0:
                at = posa_ref[at]
            block = value[q * kb : (q + 1) * kb]

            @pl.when(step < 2)
            def _(send=send, at=at, block=block):
                send[at] = block

            @pl.when(step >= 2)
            def _(keep=keep, at=at, block=block):
                keep[at] = block


def ggate_call(mids, d_gates, xord, posa):
    _, tall, model = mids.shape
    ff = d_gates.shape[2]
    kb = model // BLOCKS
    n = BLOCKS // 2
    block = lambda q: pl.BlockSpec(
        (CHUNKS, tall, kb), lambda j, xo, pa: (0, 0, xo[lax.rem(2 * j + q + n, BLOCKS)])
    )
    out = struct((n, kb, ff // 2), BF16)
    a_keep, a_send, b_keep, b_send = call(
        ggate_body,
        xord,
        posa,
        mids,
        mids,
        d_gates,
        grid=(n,),
        prefetch=2,
        in_specs=[block(0), block(1), whole(d_gates.shape)],
        out_specs=[whole(out.shape)] * 4,
        out_shape=[out] * 4,
        scratch=[pltpu.VMEM((2 * kb, CHUNKS * tall), BF16)],
        flops=2 * CHUNKS * tall * model * ff,
    )
    return [a_keep, b_keep], [a_send, b_send]


def fold(keep, send):
    for bits in ((BIT_CORE, BIT_CORE), (BIT_X, BIT_Y), (BIT_Y, BIT_X)):
        got = [flip(v, b) for v, b in zip(send, bits)]
        n = got[0].shape[0] // 2
        if n:
            send = [k[n:] + g[n:] for k, g in zip(keep, got)]
            keep = [k[:n] + g[:n] for k, g in zip(keep, got)]
        else:
            keep = [k[0].astype(F32) + g[0].astype(F32) for k, g in zip(keep, got)]
    return keep


def dres_body(dg_ref, du_ref, wg_ref, wu_ref, *outs):
    value = dot(dg_ref[0], wg_ref[...], COLS) + dot(du_ref[0], wu_ref[...], COLS)
    store_pieces(value, outs)


def dres_call(x, dg, du, w_gate, w_up):
    _, tall, ff = dg.shape
    model = w_gate.shape[0]
    rows = tall // 4
    return call(
        dres_body,
        dg,
        du,
        w_gate,
        w_up,
        grid=(model // NCOL,),
        in_specs=[spec((1, tall, ff), x, 0, 0)] * 2 + [spec((NCOL, ff), None, 0)] * 2,
        out_specs=[spec((rows, NCOL), 0, None)] * 4,
        out_shape=[struct((rows, model), t) for t in (F32, BF16, BF16, BF16)],
        flops=4 * tall * ff * model,
    )


def strips(rows, model):
    return spec((rows // STRIPS, model), None, 0)


def strips_of(x, rows, model):
    return pl.BlockSpec((rows // STRIPS, model), lambda j, *_: (x * STRIPS + j, 0))


def add_up(part_ref, value):
    @pl.when(pl.program_id(0) == 0)
    def _():
        part_ref[...] = value

    @pl.when(pl.program_id(0) > 0)
    def _():
        part_ref[...] += value


def scaled(value):
    rs = lax.rsqrt(jnp.mean(value * value, axis=1, keepdims=True) + norm_eps)
    return rs, value * rs


def total_of(refs):
    value = refs[0][...].astype(F32)
    for ref in refs[1:]:
        value = value + ref[...].astype(F32)
    return value


def post_attn_body(n, *refs):
    tok_ref, gain_ref, res_ref, mid_ref, part_ref = refs[n:]
    value = total_of(refs[:n])
    part_ref[...] = value
    _, hat = scaled(value)
    residual = tok_ref[...].astype(F32) + hat * gain_ref[...]
    res_ref[...] = residual
    mid_ref[...] = residual.astype(BF16)


def post_attn(x, terms, tokens, gain):
    rows, model = terms[0].shape
    return call(
        functools.partial(post_attn_body, len(terms)),
        *terms,
        tokens,
        gain,
        grid=(STRIPS,),
        in_specs=[strips(rows, model)] * len(terms)
        + [strips_of(x, rows, model), whole((1, model))],
        out_specs=[strips(rows, model)] * 3,
        out_shape=[struct((rows, model), t) for t in (F32, BF16, F32)],
        flops=1e6,
    )


def post_mlp_body(n, *refs):
    res_ref, cot_ref, gain_ref = refs[n : n + 3]
    out_ref, dm_ref, part_ref = refs[-3:]
    value = total_of(refs[:n])
    rs, hat = scaled(value)
    gain = gain_ref[...]
    out_ref[...] = (res_ref[...] + hat * gain).astype(BF16)
    upstream = cot_ref[...].astype(F32)
    both = upstream * hat
    add_up(part_ref, jnp.sum(both, axis=0, keepdims=True))
    mean = jnp.mean(both * gain, axis=1, keepdims=True)
    dm_ref[...] = (rs * (upstream * gain - hat * mean)).astype(BF16)


def post_mlp(x, terms, residual, cotangent, gain, prev):
    rows, model = terms[0].shape
    n = len(terms)
    extra, extra_specs, alias = chain(prev, n + 3, (0,))
    return call(
        functools.partial(post_mlp_body, n),
        *terms,
        residual,
        cotangent,
        gain,
        *extra,
        grid=(STRIPS,),
        in_specs=[strips(rows, model)] * (n + 1)
        + [strips_of(x, rows, model), whole((1, model))]
        + extra_specs,
        out_specs=[strips_of(x, rows, model), strips(rows, model), whole((1, model))],
        out_shape=[
            struct((CHUNKS * rows, model), BF16),
            struct((rows, model), BF16),
            struct((1, model), F32),
        ],
        alias=alias,
        flops=1e6,
    )


def post_bwd_body(n, *refs):
    _, attn_ref, gain_ref, dres_ref, da_ref, part_ref = refs[n:]
    value = total_of(refs[: n + 1])
    dres_ref[...] = value
    rs, hat = scaled(attn_ref[...])
    gain = gain_ref[...]
    both = value * hat
    add_up(part_ref, jnp.sum(both, axis=0, keepdims=True))
    mean = jnp.mean(both * gain, axis=1, keepdims=True)
    da_ref[...] = (rs * (value * gain - hat * mean)).astype(BF16)


def post_bwd(x, terms, cotangent, attn_part, gain):
    rows, model = terms[0].shape
    return call(
        functools.partial(post_bwd_body, len(terms)),
        *terms,
        cotangent,
        attn_part,
        gain,
        grid=(STRIPS,),
        in_specs=[strips(rows, model)] * len(terms)
        + [strips_of(x, rows, model), strips(rows, model), whole((1, model))],
        out_specs=[strips(rows, model), strips(rows, model), whole((1, model))],
        out_shape=[
            struct((rows, model), F32),
            struct((rows, model), BF16),
            struct((1, model), F32),
        ],
        flops=1e6,
    )


def last_body(n, *refs):
    refs[-1][...] = total_of(refs[: n + 1])


def last(x, terms, d_residual, prev):
    rows, model = terms[0].shape
    n = len(terms)
    extra, extra_specs, alias = chain(prev, n + 1, (0,))
    return call(
        functools.partial(last_body, n),
        *terms,
        d_residual,
        *extra,
        grid=(STRIPS,),
        in_specs=[strips(rows, model)] * (n + 1) + extra_specs,
        out_specs=[strips_of(x, rows, model)],
        out_shape=[struct((CHUNKS * rows, model), F32)],
        alias=alias,
        flops=1e6,
    )


def on_device(
    n_dp,
    tokens,
    w_query,
    w_key,
    w_value,
    w_out,
    w_gate,
    w_up,
    w_down,
    query_gain,
    key_gain,
    attn_gain,
    mlp_gain,
    cotangent,
):
    return layer(
        n_dp,
        tokens,
        w_query,
        w_key,
        w_value,
        w_out,
        w_gate,
        w_up,
        w_down,
        query_gain,
        key_gain,
        attn_gain,
        mlp_gain,
        cotangent,
    )


def layer(
    n_dp,
    tokens,
    w_query,
    w_key,
    w_value,
    w_out,
    w_gate,
    w_up,
    w_down,
    query_gain,
    key_gain,
    attn_gain,
    mlp_gain,
    cotangent,
):
    fast = n_dp == BLOCKS
    all_rows, model = tokens.shape
    rows = all_rows // CHUNKS
    length = 4 * all_rows
    heads, gain_part = query_gain.shape
    head = gain_part * n_dp
    width = heads * head
    half = 3 * width // 2
    t = lax.axis_index(TP)
    d = lax.axis_index(DP)

    third = jnp.where(t < 2, 2, 1)
    fourth = jnp.where(t < 2, 3, 0)
    sid = jnp.stack([t, t ^ 1, third, fourth]).astype(jnp.int32)
    slots = jnp.arange(4, dtype=jnp.int32)
    inv = jnp.sum(jnp.where(sid[None, :] == slots[:, None], slots[None, :], 0), axis=1)
    inv = inv.astype(jnp.int32)

    small = [query_gain.reshape(-1), key_gain.reshape(-1), attn_gain, mlp_gain]
    sizes = [s.shape[0] for s in small]
    extra = 16
    flat = jnp.concatenate(small)
    row = jnp.pad(flat[None, :], ((0, extra - 1), (0, half - flat.shape[0])))
    packed = jnp.concatenate([w_query, w_key, w_value], axis=1)
    pack_a = jnp.concatenate([packed[:, :half], row], axis=0)
    pack_b = packed[:, half:]
    if fast:
        xord = d.astype(jnp.int32) ^ jnp.array(ORDER, jnp.int32)
        a1, b1 = flip(pack_a, BIT_X), flip(pack_b, BIT_Y)
        a1 = jnp.stack([pack_a, a1])
        b1 = jnp.stack([pack_b, b1])
        a2 = jnp.concatenate([a1, flip(a1, BIT_Y)])
        b2 = jnp.stack([b1, flip(b1, BIT_X)], axis=1).reshape(4, *pack_b.shape)
        a3 = flip(a2, BIT_CORE)
        b3 = flip(b2, BIT_CORE)
        weights = (a2, a3, b2, b3)
        rel = jnp.concatenate([a2[:, -extra], a3[:, -extra]])
        place = jnp.zeros((BLOCKS,), jnp.int32).at[xord].set(jnp.arange(BLOCKS, dtype=jnp.int32))
        gains = jnp.take(rel, place, axis=0)
    else:
        xord = jnp.arange(BLOCKS, dtype=jnp.int32)
        all_a = lax.all_gather(pack_a, DP, axis=0)
        all_b = lax.all_gather(pack_b, DP, axis=0)
        wide_a = all_a[:, :-extra].reshape(BLOCKS, -1, half)
        wide_b = all_b.reshape(BLOCKS, -1, half)
        weights = (wide_a[:4], wide_a[4:], wide_b[:4], wide_b[4:])
        gains = all_a[:, -extra]
    at = [sum(sizes[:i]) for i in range(5)]

    def head_gain(values):
        values = values.reshape(n_dp, heads, gain_part).transpose(1, 0, 2)
        return values.reshape(heads, 1, head).astype(F32)

    gain_q = head_gain(gains[:, at[0] : at[1]])
    gain_k = head_gain(gains[:, at[1] : at[2]])
    gain_attn = gains[:, at[2] : at[3]].reshape(1, model).astype(F32)
    gain_mlp = gains[:, at[3] : at[4]].reshape(1, model).astype(F32)

    full_out = lax.all_gather(w_out, DP, axis=1, tiled=True)
    full_gate = lax.all_gather(w_gate, DP, axis=0, tiled=True)
    full_up = lax.all_gather(w_up, DP, axis=0, tiled=True)
    full_down = lax.all_gather(w_down, DP, axis=1, tiled=True)

    cos, sin = rope_tables(length, head)
    turns = range(CHUNKS)

    token_pieces = [line_gather(tokens[x * rows : (x + 1) * rows]) for x in turns]
    prev = None
    for x in turns:
        prev = qkv_call(x, token_pieces[x], weights, sid, xord, prev, width)
    qk, v, xs, sums = prev
    sums = [sums, *everyone(sums)]
    qrot, krot, ctx, lse, rq, rk = attn_fwd(
        inv, qk, v, sums, gain_q, gain_k, cos, sin, model
    )
    after_attn = []
    for x in turns:
        terms = line_scatter(out_call(x, ctx, full_out))
        after_attn.append(post_attn(x, terms, tokens, gain_attn))

    prev = None
    outs = None
    mlp_parts = []
    d_mlp = []
    for x in turns:
        pieces = line_gather(after_attn[x][1])
        prev = up_call(x, pieces, full_gate, full_up, sid, prev)
        terms = line_scatter(down_call(x, prev[3], full_down))
        outs, dm, part = post_mlp(
            x, terms, after_attn[x][0], cotangent, gain_mlp, outs and outs[:1]
        )
        outs = (outs,)
        d_mlp.append(dm)
        mlp_parts.append(part)
    mids, gates, ups, hiddens = prev
    layer_output = outs[0]

    prev = None
    d_res, d_attn, attn_parts = [], [], []
    for x in turns:
        pieces = line_gather(d_mlp[x])
        prev = dhid_call(x, pieces, full_down, gates, ups, sid, prev)
        terms = line_scatter(dres_call(x, prev[1], prev[2], full_gate, full_up))
        dr, da, part = post_bwd(x, terms, cotangent, after_attn[x][2], gain_attn)
        d_res.append(dr)
        d_attn.append(da)
        attn_parts.append(part)
    dms, d_gates, d_ups = prev
    flat_rows = lambda a: a.reshape(length, a.shape[2])
    grad_down = dot(flat_rows(hiddens), flat_rows(dms), ROWS, BF16)
    if fast:
        keep, send = ggate_call(mids, d_gates, xord, jnp.array((0, 2, 1, 3), jnp.int32))
        grad_gate = jnp.concatenate(fold(keep, send), axis=1)
    else:
        grad_gate = dot(flat_rows(mids), flat_rows(d_gates), ROWS, BF16)
        grad_gate = lax.psum_scatter(grad_gate, DP, scatter_dimension=0, tiled=True)
        grad_gate = grad_gate.astype(F32)
    grad_up = dot(flat_rows(mids), flat_rows(d_ups), ROWS, BF16)
    grad_down = lax.psum_scatter(grad_down, DP, scatter_dimension=1, tiled=True)
    grad_up = lax.psum_scatter(grad_up, DP, scatter_dimension=0, tiled=True)
    grad_down = grad_down.astype(F32)
    grad_up = grad_up.astype(F32)

    prev = None
    for x in turns:
        prev = dctx_call(x, line_gather(d_attn[x]), full_out, prev)
    dctx, das = prev
    lanes = 4 * rows
    gain_sums = jnp.concatenate([sum(attn_parts), sum(mlp_parts)]).reshape(-1, lanes)
    gq, gk, dv, head_gains, dots = attn_bwd(
        inv, qrot, krot, v, dctx, ctx, lse, qk, rq, rk, gain_q, gain_k, cos, sin, gain_sums
    )
    dots = [dots, *everyone(dots)]
    grad_tokens = None
    for x in turns:
        if x == 0:
            sources = (*dots, gq, gk, dv, qk, rq, rk)
            *parts, dqkv = dinput_call(x, sources, weights, sid, xord, model)
        else:
            parts = dinput_call(x, (dqkv,), weights, sid, xord, model)
        terms = line_scatter(parts)
        grad_tokens = last(x, terms, d_res[x], grad_tokens)
    grad_tokens = grad_tokens[0]

    gain_sums = sum(a[8 * CHUNKS :] for a in dots).reshape(2, n_dp, -1)

    def spread(values):
        values = values.reshape(heads, n_dp, gain_part).transpose(1, 0, 2)
        return values.reshape(n_dp, heads * gain_part)

    gain_rows = jnp.concatenate(
        [spread(head_gains[:, 0]), spread(head_gains[:, 1]), gain_sums[0], gain_sums[1]], axis=1
    )
    cols = half + model // BLOCKS
    gain_rows = jnp.pad(gain_rows, ((0, 0), (0, cols - gain_rows.shape[1])))
    wgrad = lambda part, rows, posa: wgrad_call(
        part, xs, dqkv, ctx, das, rows, xord, jnp.array(posa, jnp.int32)
    )
    if fast:
        packed_gains = jnp.pad(gain_rows[:, None, :], ((0, 0), (0, extra - 1), (0, 0)))
        packed_gains = packed_gains.astype(BF16)
        send = wgrad(1, packed_gains, (0, 2, 1, 3))
        keep = wgrad(0, packed_gains, (0, 2, 1, 3))
        g_a, g_b = fold(keep, send)
        gain_row = g_a[-extra]
        g_a = g_a[:-extra]
        grad_out = jnp.concatenate([g_a[:, half:], g_b[:, half:]])
        grad_qkv = jnp.concatenate([g_a[:, :half], g_b[:, :half]], axis=1)
    else:
        packed_gains = jnp.zeros((BLOCKS, extra, cols), BF16)
        low = wgrad(0, packed_gains, (0, 1, 2, 3))
        high = wgrad(1, packed_gains, (0, 1, 2, 3))
        g_a = jnp.concatenate([low[0], high[0]])[:, :-extra]
        g_b = jnp.concatenate([low[1], high[1]])
        grad_out = jnp.concatenate([g_a[:, :, half:], g_b[:, :, half:]], axis=1)
        grad_out = grad_out.transpose(1, 0, 2).reshape(width, model)
        grad_out = lax.psum_scatter(grad_out, DP, scatter_dimension=1, tiled=True)
        g_a = g_a[:, :, :half].reshape(model, half)
        g_b = g_b[:, :, :half].reshape(model, half)
        g_a = lax.psum_scatter(g_a, DP, scatter_dimension=0, tiled=True)
        g_b = lax.psum_scatter(g_b, DP, scatter_dimension=0, tiled=True)
        gain_row = lax.psum_scatter(gain_rows, DP, scatter_dimension=0, tiled=True)[0]
        grad_qkv = jnp.concatenate([g_a, g_b], axis=1).astype(F32)
    gain_row = gain_row.astype(F32)
    return (
        layer_output,
        grad_tokens,
        grad_qkv[:, :width],
        grad_qkv[:, width : 2 * width],
        grad_qkv[:, 2 * width :],
        grad_out.astype(F32),
        grad_gate,
        grad_up,
        grad_down,
        gain_row[at[0] : at[1]].reshape(heads, gain_part),
        gain_row[at[1] : at[2]].reshape(heads, gain_part),
        gain_row[at[2] : at[3]],
        gain_row[at[3] : at[4]],
    )


def solution(mesh):
    in_specs = (
        P((DP, TP), None),
        P(DP, TP),
        P(DP, TP),
        P(DP, TP),
        P(TP, DP),
        P(DP, TP),
        P(DP, TP),
        P(TP, DP),
        P(TP, DP),
        P(TP, DP),
        P(DP),
        P(DP),
        P((DP, TP), None),
    )
    out_specs = (
        P((DP, TP), None),
        P((DP, TP), None),
        P(DP, TP),
        P(DP, TP),
        P(DP, TP),
        P(TP, DP),
        P(DP, TP),
        P(DP, TP),
        P(TP, DP),
        P(TP, DP),
        P(TP, DP),
        P(DP),
        P(DP),
    )
    assert mesh.shape[TP] == 4
    return jax.shard_map(
        functools.partial(on_device, mesh.shape[DP]),
        mesh=mesh,
        in_specs=in_specs,
        out_specs=out_specs,
        check_vma=False,
    )
```
